256 devices in a mesh: lon: 32 (over y, z), lat: 8 (over x, core).
Axes of the slice: x: 4, y: 4, z: 8, core: 2. Of those that a mesh axis runs over, the one named last changes fastest.
Arguments:
- fields: float32 [129, 6, 128, 1024], P(None, None, 'lat', 'lon'), may hold values from -38 to 38
Outputs:
- koopman_modes: float32 [30, 128, 1024, 128], P(None, 'lat', 'lon')
- forward_operator: float32 [128, 128], replicated
- backward_operator: float32 [128, 128], replicated
The draws below stay inside these ranges and needn't reach their ends.
All inputs are finite; a program needn't handle non-finite values.
Results may differ from the reference program's by a relative error of at most 0.0001.
Values sent between devices are 32-bit elements; how exact they have to be, the bound alone decides.
A program may use at most 64 MiB of HBM per device.

```python
import math
import jax
import jax.numpy as jnp
from jax import lax

CH = 6
STATES = 129
NLAT = 128
NLON = 1024


def draw_fields(key, part):
    noise_key = jax.random.fold_in(jax.random.fold_in(key, 7), 0)
    noise_shape = (STATES + 1, CH, NLAT, NLON)
    noise = jnp.clip(jax.random.normal(noise_key, noise_shape, jnp.float32), -4.0, 4.0)
    lat_pos = jnp.arange(NLAT, dtype=jnp.float32) / max(NLAT - 1, 1)
    lon_pos = jnp.arange(NLON, dtype=jnp.float32) / NLON
    memory = (0.2 + 0.6 * lat_pos)[:, None]
    amplitude = (3.0 ** (0.5 * lat_pos))[:, None] * (3.0 ** (0.5 + 0.5 * jnp.sin(2.0 * math.pi * lon_pos)))[None, :]
    return amplitude * (noise[1:] + memory * noise[:-1])


def setup_inputs(seed: int = 0) -> dict:
    key_list = jax.random.split(jax.random.key(seed), 2)
    return {
        "fields": draw_fields(jax.random.fold_in(key_list[1], 71), 0),
    }


def build_slabs(fields):
    north_cells = jnp.pad(fields, ((0, 0), (0, 0), (1, 0), (0, 0)))[:, :, :-1]
    south_cells = jnp.pad(fields, ((0, 0), (0, 0), (0, 1), (0, 0)))[:, :, 1:]
    west_cells = jnp.roll(fields, 1, axis=3)
    east_cells = jnp.roll(fields, -1, axis=3)
    return [fields] + [fields * neighbour for neighbour in (north_cells, south_cells, west_cells, east_cells)]

def reduced_operators(upper_factor, gram_total):
    snap_count = upper_factor.shape[0] - 1
    head_block = upper_factor[:snap_count, :snap_count]
    forward_operator = jax.scipy.linalg.solve_triangular(head_block.T, upper_factor[:snap_count, 1:].T, lower=True).T
    back_factor = jnp.linalg.cholesky(gram_total[1:, 1:])
    mixed_block = jax.scipy.linalg.solve_triangular(back_factor, gram_total[1:, :snap_count], lower=True)
    backward_operator = jax.scipy.linalg.solve_triangular(back_factor, mixed_block.T, lower=True).T
    return (forward_operator, backward_operator)

def reference(fields):
    states = fields.shape[0]
    snap_count = states - 1
    slab_list = build_slabs(fields)
    rows_total = 5 * CH * NLAT * NLON
    gram_total = jnp.zeros((states, states), jnp.float32)
    for feature_slab in slab_list:
        flat_rows = feature_slab.reshape(states, -1)
        gram_total = gram_total + jnp.dot(flat_rows, flat_rows.T, precision=lax.Precision.HIGHEST)
    gram_total = gram_total / rows_total
    upper_factor = jnp.linalg.cholesky(gram_total).T
    forward_operator, backward_operator = reduced_operators(upper_factor, gram_total)
    head_block = upper_factor[:snap_count, :snap_count]
    mode_parts = []
    for feature_slab in slab_list:
        flat_rows = feature_slab.reshape(states, -1)[:snap_count]
        solved = jax.scipy.linalg.solve_triangular(head_block.T, flat_rows, lower=True)
        mode_parts.append(solved.reshape(snap_count, CH, NLAT, NLON).transpose(1, 2, 3, 0))
    koopman_modes = jnp.concatenate(mode_parts, axis=0)
    return (koopman_modes, forward_operator, backward_operator)
```

```python
import functools

import jax
import jax.numpy as jnp
from jax import lax
from jax.experimental import pallas as pl
from jax.experimental.pallas import tpu as pltpu
from jax.sharding import PartitionSpec as P

F32, BF16 = jnp.float32, jnp.bfloat16
MESH = pl.DeviceIdType.MESH
CHANNELS, ROWS, COLS, LANES = 6, 16, 32, 128


def split_pair(value):
    high = value.astype(BF16)
    low = (value - high.astype(F32)).astype(BF16)
    return jnp.concatenate([high, low], axis=-1)


def flat(value):
    return value.reshape(-1, value.shape[-1])


def iota(shape, dim):
    return lax.broadcasted_iota(jnp.int32, shape, dim)


def self_product(value):
    pair = split_pair(value)
    return lax.dot_general(pair, pair, (((0,), (0,)), ((), ())), preferred_element_type=F32)


def gram_kernel(
    sizes, cells_total, fields,
    gram_out, north_out, south_out, west_out, east_out,
    body, last_raw, last, edge, north, south, west, east,
    pack_row, pack_col, pack_own, got_row, got_col,
    acc_one, acc_two, part, lat_buf, y_buf, z_buf, all_buf,
    load_sem, halo_send, halo_recv, lat_send, lat_recv, y_send, y_recv, z_send, z_recv, all_send, all_recv,
):
    n_lat, n_y, n_z = sizes
    n_lon = n_y * n_z
    lat, lon = lax.axis_index("lat"), lax.axis_index("lon")
    y, z = lon // n_z, lon % n_z
    above, below = lon - 1 + n_lon, lon + 1
    west_id, east_id = {"lon": above % n_lon}, {"lon": below % n_lon}

    def lat_peer(step):
        return (lat + step) % n_lat

    def y_peer(step):
        return (y + step) % n_y

    def z_peer(step):
        return (z + step) % n_z

    barrier = pltpu.get_barrier_semaphore()
    greeted = [west_id, east_id]
    greeted += [{"lat": lat_peer(step)} for step in range(1, n_lat)]
    greeted += [{"lon": y_peer(step) * n_z + z} for step in range(1, n_y)]
    greeted += [{"lon": y * n_z + z_peer(step)} for step in range(1, n_z)]
    for peer in greeted:
        pl.semaphore_signal(barrier, inc=1, device_id=peer, device_id_type=MESH)

    main = pl.ds(0, LANES)
    loads = [
        pltpu.make_async_copy(fields.at[:, :, :, main], body.at[:, pl.ds(0, ROWS), pl.ds(0, COLS), :], load_sem.at[0]),
        pltpu.make_async_copy(fields.at[:, :, :, pl.ds(LANES, 1)], last_raw, load_sem.at[1]),
        pltpu.make_async_copy(fields.at[:, :, COLS - 1, main], edge, load_sem.at[2]),
    ]
    for copy in loads:
        copy.start()

    body[:, ROWS : ROWS + 1, 0:COLS, :] = jnp.zeros((CHANNELS, 1, COLS, LANES), F32)
    body[:, :, COLS : COLS + 8, :] = jnp.zeros((CHANNELS, ROWS + 1, 8, LANES), F32)
    last[:, ROWS : ROWS + 1, 0:COLS, :] = jnp.zeros((CHANNELS, 1, COLS, LANES), F32)
    last[:, :, COLS : COLS + 8, :] = jnp.zeros((CHANNELS, ROWS + 1, 8, LANES), F32)
    acc_one[...] = jnp.zeros_like(acc_one)
    acc_two[...] = jnp.zeros_like(acc_two)

    loads[1].wait()
    for c in range(CHANNELS):
        last[c, 0:ROWS, 0:COLS, :] = jnp.broadcast_to(last_raw[c], (ROWS, COLS, LANES))

    lane8, sub8 = iota((8, LANES), 1), iota((8, LANES), 0)
    packed = jnp.zeros((8, LANES), F32)
    for c in range(CHANNELS):
        for t in range(COLS // 8):
            packed = jnp.where(lane8 == c * 4 + t, last[c, 0, 8 * t : 8 * t + 8, :], packed)
    pack_row[...] = packed

    def pack_column(j):
        packed = jnp.zeros((8, LANES), F32)
        for c in range(CHANNELS):
            for i in range(ROWS):
                one = jnp.broadcast_to(last[c, i, j : j + 1, :], (8, LANES))
                packed = jnp.where((lane8 == c * 2 + i // 8) & (sub8 == i % 8), one, packed)
        return packed

    pack_col[...] = pack_column(0)
    pack_own[...] = pack_column(COLS - 1)

    loads[0].wait()
    loads[2].wait()

    def sums(value, other):
        return (value * other).reshape(-1, 8, LANES).sum(axis=0)

    def plain(c, carry):
        cross, own = carry
        value = flat(body[c, 0:ROWS, 0:COLS, :])
        tail = flat(last[c, 0:ROWS, 0:COLS, :])
        acc_one[...] += self_product(value)
        return cross + sums(value, tail), own + sums(tail, tail)

    zero = jnp.zeros((8, LANES), F32)
    cross_one, own_one = lax.fori_loop(0, CHANNELS, plain, (zero, zero))

    pl.semaphore_wait(barrier, len(greeted))

    def remote(source, target, index, peer):
        return pltpu.make_async_remote_copy(
            source, target, halo_send.at[index], halo_recv.at[index], device_id=peer, device_id_type=MESH
        )

    lat_up = {"lat": lax.max(lat - 1, 0)}
    lat_down = {"lat": lax.min(lat + 1, n_lat - 1)}
    east_copies = [
        remote(fields.at[:, :, 0, main], east, 0, west_id),
        remote(pack_col, got_col, 1, west_id),
    ]
    south_copies = [
        remote(fields.at[:, 0, :, main], south, 2, lat_up),
        remote(pack_row, got_row, 3, lat_up),
    ]
    west_copy = remote(fields.at[:, :, COLS - 1, main], west, 4, east_id)
    north_copy = remote(fields.at[:, ROWS - 1, :, main], north, 5, lat_down)

    @pl.when(lat > 0)
    def _():
        for copy in south_copies:
            copy.start()

    for copy in east_copies:
        copy.start()

    @pl.when(lat < n_lat - 1)
    def _():
        north_copy.start()

    west_copy.start()

    def crossed(c, carry):
        cross, own = carry
        value = body[c, 0:ROWS, 0:COLS, :]
        tail = last[c, 0:ROWS, 0:COLS, :]
        lower = flat(value * body[c, 1 : ROWS + 1, 0:COLS, :])
        right = flat(value * body[c, 0:ROWS, 1 : COLS + 1, :])
        tail_lower = flat(tail * last[c, 1 : ROWS + 1, 0:COLS, :])
        tail_right = flat(tail * last[c, 0:ROWS, 1 : COLS + 1, :])
        acc_two[...] += self_product(lower)
        acc_two[...] += self_product(right)
        cross += sums(lower, tail_lower) + sums(right, tail_right)
        own += sums(tail_lower, tail_lower) + sums(tail_right, tail_right)
        return cross, own

    cross_two, own_two = lax.fori_loop(0, CHANNELS, crossed, (zero, zero))

    @pl.when(lat < n_lat - 1)
    def _():
        for copy in south_copies:
            copy.wait_recv()

    for copy in east_copies:
        copy.wait_recv()

    @pl.when(lat == n_lat - 1)
    def _():
        south[...] = jnp.zeros_like(south)
        got_row[...] = jnp.zeros_like(got_row)

    @pl.when(lat == 0)
    def _():
        north[...] = jnp.zeros_like(north)

    def spread(packed, lane):
        return jnp.broadcast_to(packed[:, lane : lane + 1], (8, LANES))

    row_packed, col_packed, own_packed = got_row[...], got_col[...], pack_own[...]
    tail_row = jnp.concatenate([spread(row_packed, lane) for lane in range(CHANNELS * 4)], axis=0)
    tail_row = tail_row * flat(last[:, ROWS - 1, 0:COLS, :])
    tail_col = [spread(col_packed, lane) * spread(own_packed, lane) for lane in range(CHANNELS * 2)]
    tails = jnp.concatenate([tail_row] + tail_col, axis=0)
    border = jnp.concatenate(
        [flat(body[:, ROWS - 1, 0:COLS, :] * south[...]), flat(edge[...] * east[...])], axis=0
    )
    acc_two[...] += self_product(border)
    cross_two += sums(border, tails)
    own_two += sums(tails, tails)

    total = acc_one[...] + 2.0 * acc_two[...]
    scale = 1.0 / cells_total
    full = (total[:LANES, :LANES] + total[LANES:, LANES:]) + (total[:LANES, LANES:] + total[LANES:, :LANES])
    full = full * scale
    cross = (cross_one + 2.0 * cross_two).sum(axis=0, keepdims=True) * scale
    own = (own_one + 2.0 * own_two).sum(axis=0, keepdims=True) * scale

    half = LANES // 2
    top, bottom = full[:half], full[half:]
    row, lane = iota((half, LANES), 0), iota((half, LANES), 1)
    folded = jnp.where((lane < half) & (row < lane), pltpu.roll(bottom, half, 1), top)
    diagonal = jnp.where(lane == row + half, bottom, 0.0).sum(axis=0, keepdims=True)
    extra = jnp.where(iota((1, LANES), 1) < half, own, diagonal)
    rows = half // n_lat
    for owner in range(n_lat):
        part[owner, 0:rows, :] = folded[owner * rows : (owner + 1) * rows]
        tail = cross if owner == 0 else extra if owner == 1 else jnp.zeros((1, LANES), F32)
        part[owner, rows : rows + 1, :] = tail

    def exchange(count, me, peer_of, device_of, source_of, buf, send, recv):
        copies = [
            pltpu.make_async_remote_copy(
                source_of(peer_of(step)), buf.at[me], send.at[step], recv.at[step],
                device_id=device_of(peer_of(step)), device_id_type=MESH,
            )
            for step in range(1, count)
        ]
        for copy in copies:
            copy.start()
        arrivals = [
            pltpu.make_async_remote_copy(
                buf.at[me], buf.at[peer_of(count - step)], send.at[step], recv.at[step],
                device_id=device_of(peer_of(step)), device_id_type=MESH,
            )
            for step in range(1, count)
        ]
        for copy in arrivals:
            copy.wait_recv()
        return copies

    def added(buf, count):
        result = buf[0]
        for index in range(1, count):
            result = result + buf[index]
        return result

    lat_buf[lat] = part[lat]
    pending = exchange(
        n_lat, lat, lat_peer, lambda p: {"lat": p}, lambda p: part.at[p], lat_buf, lat_send, lat_recv
    )
    y_buf[y] = added(lat_buf, n_lat)
    pending += exchange(
        n_y, y, y_peer, lambda p: {"lon": p * n_z + z}, lambda p: y_buf.at[y], y_buf, y_send, y_recv
    )
    z_buf[z] = added(y_buf, n_y)
    pending += exchange(
        n_z, z, z_peer, lambda p: {"lon": y * n_z + p}, lambda p: z_buf.at[z], z_buf, z_send, z_recv
    )
    all_buf[lat] = added(z_buf, n_z)
    pending += exchange(
        n_lat, lat, lat_peer, lambda p: {"lat": p}, lambda p: all_buf.at[lat], all_buf, all_send, all_recv
    )
    gram_out[...] = all_buf[...]

    @pl.when(lat > 0)
    def _():
        north_copy.wait_recv()
        for copy in south_copies:
            copy.wait_send()

    @pl.when(lat < n_lat - 1)
    def _():
        north_copy.wait_send()

    west_copy.wait_recv()
    for copy in [west_copy] + east_copies + pending:
        copy.wait_send()
    north_out[...] = north[...]
    south_out[...] = south[...]
    west_out[...] = west[...]
    east_out[...] = east[...]


def gram_call(fields, n_lat, n_lon):
    n_z = 8 if n_lon % 32 == 0 else max(n_lon // 2, 1)
    n_y = n_lon // n_z
    rows = LANES // 2 // n_lat + 1
    cells_total = 5 * CHANNELS * ROWS * n_lat * COLS * n_lon
    row_shape, col_shape = (CHANNELS, COLS, LANES), (CHANNELS, ROWS, LANES)
    chunk = (rows, LANES)
    dma = pltpu.SemaphoreType.DMA
    shapes = [(n_lat,) + chunk, row_shape, row_shape, col_shape, col_shape]
    vmem = pl.BlockSpec(memory_space=pltpu.VMEM)
    return pl.pallas_call(
        functools.partial(gram_kernel, (n_lat, n_y, n_z), cells_total),
        out_shape=[jax.ShapeDtypeStruct(shape, F32) for shape in shapes],
        in_specs=[pl.BlockSpec(memory_space=pl.ANY)],
        out_specs=[vmem] * 5,
        scratch_shapes=[
            pltpu.VMEM((CHANNELS, ROWS + 1, COLS + 8, LANES), F32),
            pltpu.VMEM((CHANNELS, ROWS, COLS, 1), F32),
            pltpu.VMEM((CHANNELS, ROWS + 1, COLS + 8, LANES), F32),
            pltpu.VMEM(col_shape, F32),
            pltpu.VMEM(row_shape, F32),
            pltpu.VMEM(row_shape, F32),
            pltpu.VMEM(col_shape, F32),
            pltpu.VMEM(col_shape, F32),
        ]
        + [pltpu.VMEM((8, LANES), F32)] * 5
        + [pltpu.VMEM((2 * LANES, 2 * LANES), F32)] * 2
        + [
            pltpu.VMEM((n_lat,) + chunk, F32),
            pltpu.VMEM((n_lat,) + chunk, F32),
            pltpu.VMEM((n_y,) + chunk, F32),
            pltpu.VMEM((n_z,) + chunk, F32),
            pltpu.VMEM((n_lat,) + chunk, F32),
            dma((3,)),
            dma((6,)), dma((6,)),
            dma((n_lat,)), dma((n_lat,)),
            dma((n_y,)), dma((n_y,)),
            dma((n_z,)), dma((n_z,)),
            dma((n_lat,)), dma((n_lat,)),
        ],
        compiler_params=pltpu.CompilerParams(
            collective_id=0, has_side_effects=True, vmem_limit_bytes=40 << 20
        ),
    )(fields)


def unfolded(gram):
    n_lat, rows, _ = gram.shape
    half = LANES // 2
    folded = jnp.concatenate([gram[owner, : rows - 1, :] for owner in range(n_lat)], axis=0)
    cross, extra = gram[0, rows - 1 : rows, :], gram[1, rows - 1 : rows, :]
    row, lane = iota((half, LANES), 0), iota((half, LANES), 1)
    top = jnp.where((lane < half) & (row <= lane), 0.0, folded)
    bottom = jnp.where((lane >= half) & (row < lane - half), pltpu.roll(folded, half, 1), 0.0)
    once = jnp.concatenate([top, bottom], axis=0)
    diagonal = jnp.concatenate(
        [jnp.where(lane == row, folded, 0.0), jnp.where(lane == row + half, jnp.broadcast_to(extra, (half, LANES)), 0.0)],
        axis=0,
    )
    full = once + once.T + diagonal
    row, lane = iota((LANES, LANES), 0), iota((LANES, LANES), 1)

    def column(line):
        return jnp.where(row == lane, jnp.broadcast_to(line, (LANES, LANES)), 0.0).sum(axis=1, keepdims=True)

    corner = extra[:, 0:1]
    shifted = pltpu.roll(pltpu.roll(full, LANES - 1, 0), LANES - 1, 1)
    line = jnp.where(iota((1, LANES), 1) == LANES - 1, corner, pltpu.roll(cross, LANES - 1, 1))
    shifted = jnp.where(lane == LANES - 1, column(line), shifted)
    shifted = jnp.where(row == LANES - 1, jnp.broadcast_to(line, (LANES, LANES)), shifted)
    identity = jnp.where(row == lane, 1.0, 0.0)
    first = jnp.where(lane == LANES - 1, column(cross), identity)
    low = jnp.where(row == LANES - 1, cross[:, 0:1], pltpu.roll(full, LANES - 1, 0)[:, 0:1])
    second = jnp.where(lane == LANES - 1, low, identity)
    return (full, first), (shifted, second)


def eliminate(b, work, c):
    start = pl.multiple_of(b * 8, 8)
    left = work[c, pl.ds(start, 8), 0:LANES]
    right = work[c, pl.ds(start, 8), LANES : 2 * LANES]
    block = pltpu.roll(left, (LANES - start) % LANES, 1)
    columns = [jnp.broadcast_to(block[:, j : j + 1], (8, LANES)) for j in range(8)]
    entry = {}
    for i in range(8):
        for j in range(i, 8):
            entry[i, j] = jnp.broadcast_to(columns[j][i : i + 1, :], (8, LANES))
    left_rows = [jnp.broadcast_to(left[i : i + 1, :], (8, LANES)) for i in range(8)]
    right_rows = [jnp.broadcast_to(right[i : i + 1, :], (8, LANES)) for i in range(8)]
    inverse = []
    for k in range(8):
        inverse.append(1.0 / entry[k, k])
        for i in range(k + 1, 8):
            factor = entry[k, i] * inverse[k]
            for j in range(i, 8):
                entry[i, j] = entry[i, j] - factor * entry[k, j]
            left_rows[i] = left_rows[i] - factor * left_rows[k]
            right_rows[i] = right_rows[i] - factor * right_rows[k]
    sub, lane = iota((8, LANES), 0), iota((8, LANES), 1)

    def gathered(rows):
        result = rows[0]
        for k in range(1, 8):
            result = jnp.where(sub == k, rows[k], result)
        return result

    pivots = gathered(inverse)
    done = gathered(left_rows)
    factors = jnp.where(lane >= start + 8, done * pivots, 0.0).T
    root = jnp.sqrt(pivots)
    work[c, pl.ds(start, 8), 0:LANES] = done * root
    work[c, pl.ds(start, 8), LANES : 2 * LANES] = gathered(right_rows) * root
    for t in range(16):
        rows = slice(8 * t, 8 * t + 8)
        lower_left = work[c, rows, 0:LANES]
        lower_right = work[c, rows, LANES : 2 * LANES]
        for k in range(8):
            factor = jnp.broadcast_to(factors[rows, k : k + 1], (8, LANES))
            lower_left = lower_left - factor * left_rows[k]
            lower_right = lower_right - factor * right_rows[k]
        work[c, rows, 0:LANES] = lower_left
        work[c, rows, LANES : 2 * LANES] = lower_right


def accurate(left, right):
    return lax.dot_general(
        left, right, (((1,), (1,)), ((), ())), precision=lax.Precision.HIGHEST, preferred_element_type=F32
    )


def modes_kernel(
    fields, gram, north, south, west, east, modes, forward, backward,
    body, work, weights, plain, lower, left, right, load_sem, store_sem,
):
    main = pl.ds(0, LANES)
    inner, across = pl.ds(1, ROWS), pl.ds(8, COLS)
    loads = [
        pltpu.make_async_copy(fields.at[:, :, :, main], body.at[:, inner, across, :], load_sem.at[0]),
        pltpu.make_async_copy(north, body.at[:, 0, across, :], load_sem.at[1]),
        pltpu.make_async_copy(south, body.at[:, ROWS + 1, across, :], load_sem.at[2]),
        pltpu.make_async_copy(west, body.at[:, inner, 7, :], load_sem.at[3]),
        pltpu.make_async_copy(east, body.at[:, inner, 8 + COLS, :], load_sem.at[4]),
    ]
    for copy in loads:
        copy.start()

    for c, (matrix, extended) in enumerate(unfolded(gram[...])):
        work[c, :, 0:LANES] = matrix
        work[c, :, LANES : 2 * LANES] = extended

    def step(b, carry):
        eliminate(b, work, 0)
        eliminate(b, work, 1)
        return carry

    lax.fori_loop(0, 16, step, 0)

    row, lane = iota((LANES, LANES), 0), iota((LANES, LANES), 1)

    def parts(c):
        factor, extended = work[c, :, 0:LANES], work[c, :, LANES : 2 * LANES]
        corner = jnp.where((row == LANES - 1) & (lane == LANES - 1), 1.0 / factor, 0.0)
        return factor, extended, jnp.where(lane == LANES - 1, corner, extended)

    factor, extended, inverse = parts(0)
    mixing = inverse.T
    high = mixing.astype(BF16)
    low = (mixing - high.astype(F32)).astype(BF16)
    line = jnp.concatenate([high, low], axis=1)
    weights[...] = jnp.concatenate([line, line], axis=0)

    for copy in loads:
        copy.wait()

    def mixed(value):
        both = jnp.dot(split_pair(value), weights[...], preferred_element_type=F32)
        return both[:, :LANES] + both[:, LANES:]

    def stores(c):
        return [
            pltpu.make_async_copy(plain.at[c], modes.at[c], store_sem.at[0, c]),
            pltpu.make_async_copy(lower.at[c, pl.ds(0, ROWS)], modes.at[CHANNELS + c], store_sem.at[1, c]),
            pltpu.make_async_copy(lower.at[c, pl.ds(1, ROWS)], modes.at[2 * CHANNELS + c], store_sem.at[2, c]),
            pltpu.make_async_copy(left.at[c], modes.at[3 * CHANNELS + c], store_sem.at[3, c]),
            pltpu.make_async_copy(right.at[c], modes.at[4 * CHANNELS + c], store_sem.at[4, c]),
        ]

    def channel(c, carry):
        value = body[c, 1 : ROWS + 1, 8 : 8 + COLS, :]
        shape = (ROWS, COLS, LANES)
        plain[c] = mixed(flat(value)).reshape(shape)
        pairs = body[c, 0 : ROWS + 1, 8 : 8 + COLS, :] * body[c, 1 : ROWS + 2, 8 : 8 + COLS, :]
        lower[c] = mixed(flat(pairs)).reshape((ROWS + 1, COLS, LANES))
        left[c] = mixed(flat(value * body[c, 1 : ROWS + 1, 7 : 7 + COLS, :])).reshape(shape)
        right[c] = mixed(flat(value * body[c, 1 : ROWS + 1, 9 : 9 + COLS, :])).reshape(shape)
        for copy in stores(c):
            copy.start()
        return carry

    lax.fori_loop(0, CHANNELS, channel, 0)

    shifted = jnp.where(lane == LANES - 1, extended, pltpu.roll(factor, LANES - 1, 1))
    forward[...] = accurate(shifted, inverse)
    factor, extended, inverse = parts(1)
    mixed_block = jnp.where(lane == 0, pltpu.roll(extended, 1, 1), pltpu.roll(factor, 1, 1))
    backward[...] = accurate(mixed_block, inverse)

    def finish(c, carry):
        for copy in stores(c):
            copy.wait()
        return carry

    lax.fori_loop(0, CHANNELS, finish, 0)


def modes_call(fields, gram, north, south, west, east):
    shape = (CHANNELS, ROWS, COLS, LANES)
    any_space = pl.BlockSpec(memory_space=pl.ANY)
    vmem = pl.BlockSpec(memory_space=pltpu.VMEM)
    return pl.pallas_call(
        modes_kernel,
        out_shape=[
            jax.ShapeDtypeStruct((5 * CHANNELS, ROWS, COLS, LANES), F32),
            jax.ShapeDtypeStruct((LANES, LANES), F32),
            jax.ShapeDtypeStruct((LANES, LANES), F32),
        ],
        in_specs=[any_space, vmem, any_space, any_space, any_space, any_space],
        out_specs=[any_space, vmem, vmem],
        scratch_shapes=[
            pltpu.VMEM((CHANNELS, ROWS + 2, COLS + 16, LANES), F32),
            pltpu.VMEM((2, LANES, 2 * LANES), F32),
            pltpu.VMEM((2 * LANES, 2 * LANES), BF16),
            pltpu.VMEM(shape, F32),
            pltpu.VMEM((CHANNELS, ROWS + 1, COLS, LANES), F32),
            pltpu.VMEM(shape, F32),
            pltpu.VMEM(shape, F32),
            pltpu.SemaphoreType.DMA((5,)),
            pltpu.SemaphoreType.DMA((5, CHANNELS)),
        ],
        compiler_params=pltpu.CompilerParams(vmem_limit_bytes=40 << 20),
    )(fields, gram, north, south, west, east)


def shards(fields):
    cells = fields.transpose(1, 2, 3, 0)
    gram, north, south, west, east = gram_call(cells, lax.axis_size("lat"), lax.axis_size("lon"))
    return tuple(modes_call(cells, gram, north, south, west, east))


def solution(mesh):
    return jax.shard_map(
        shards,
        mesh=mesh,
        in_specs=(P(None, None, "lat", "lon"),),
        out_specs=(P(None, "lat", "lon", None), P(), P()),
        check_vma=False,
    )
```

```python
import functools

import jax
import jax.numpy as jnp
from jax import lax
from jax.experimental import pallas as pl
from jax.experimental.pallas import tpu as pltpu
from jax.sharding import PartitionSpec as P

F32, BF16 = jnp.float32, jnp.bfloat16
MESH = pl.DeviceIdType.MESH
CHANNELS, ROWS, COLS, LANES = 6, 16, 32, 128


def split_pair(value):
    high = value.astype(BF16)
    low = (value - high.astype(F32)).astype(BF16)
    return jnp.concatenate([high, low], axis=-1)


def flat(value):
    return value.reshape(-1, value.shape[-1])


def iota(shape, dim):
    return lax.broadcasted_iota(jnp.int32, shape, dim)


def self_product(value):
    pair = split_pair(value)
    return lax.dot_general(pair, pair, (((0,), (0,)), ((), ())), preferred_element_type=F32)


def gram_kernel(
    sizes, cells_total, fields,
    gram_out, north_out, south_out, west_out, east_out,
    body, last_raw, last, edge, north, south, west, east,
    pack_row, pack_col, pack_own, got_row, got_col,
    acc_one, acc_two, part, lat_buf, y_buf, z_buf, all_buf,
    load_sem, halo_send, halo_recv, lat_send, lat_recv, y_send, y_recv, z_send, z_recv, all_send, all_recv,
):
    n_lat, n_y, n_z = sizes
    n_lon = n_y * n_z
    lat, lon = lax.axis_index("lat"), lax.axis_index("lon")
    y, z = lon // n_z, lon % n_z
    above, below = lon - 1 + n_lon, lon + 1
    west_id, east_id = {"lon": above % n_lon}, {"lon": below % n_lon}

    def lat_peer(step):
        return (lat + step) % n_lat

    def y_peer(step):
        return (y + step) % n_y

    def z_peer(step):
        return (z + step) % n_z

    barrier = pltpu.get_barrier_semaphore()
    greeted = [west_id, east_id]
    greeted += [{"lat": lat_peer(step)} for step in range(1, n_lat)]
    greeted += [{"lon": y_peer(step) * n_z + z} for step in range(1, n_y)]
    greeted += [{"lon": y * n_z + z_peer(step)} for step in range(1, n_z)]
    for peer in greeted:
        pl.semaphore_signal(barrier, inc=1, device_id=peer, device_id_type=MESH)

    main = pl.ds(0, LANES)
    loads = [
        pltpu.make_async_copy(fields.at[:, :, :, main], body.at[:, pl.ds(0, ROWS), pl.ds(0, COLS), :], load_sem.at[0]),
        pltpu.make_async_copy(fields.at[:, :, :, pl.ds(LANES, 1)], last_raw, load_sem.at[1]),
        pltpu.make_async_copy(fields.at[:, :, COLS - 1, main], edge, load_sem.at[2]),
    ]
    for copy in loads:
        copy.start()

    body[:, ROWS : ROWS + 1, 0:COLS, :] = jnp.zeros((CHANNELS, 1, COLS, LANES), F32)
    body[:, :, COLS : COLS + 8, :] = jnp.zeros((CHANNELS, ROWS + 1, 8, LANES), F32)
    last[:, ROWS : ROWS + 1, 0:COLS, :] = jnp.zeros((CHANNELS, 1, COLS, LANES), F32)
    last[:, :, COLS : COLS + 8, :] = jnp.zeros((CHANNELS, ROWS + 1, 8, LANES), F32)
    acc_one[...] = jnp.zeros_like(acc_one)
    acc_two[...] = jnp.zeros_like(acc_two)

    loads[1].wait()
    for c in range(CHANNELS):
        last[c, 0:ROWS, 0:COLS, :] = jnp.broadcast_to(last_raw[c], (ROWS, COLS, LANES))

    lane8, sub8 = iota((8, LANES), 1), iota((8, LANES), 0)
    packed = jnp.zeros((8, LANES), F32)
    for c in range(CHANNELS):
        for t in range(COLS // 8):
            packed = jnp.where(lane8 == c * 4 + t, last[c, 0, 8 * t : 8 * t + 8, :], packed)
    pack_row[...] = packed

    def pack_column(j):
        packed = jnp.zeros((8, LANES), F32)
        for c in range(CHANNELS):
            for i in range(ROWS):
                one = jnp.broadcast_to(last[c, i, j : j + 1, :], (8, LANES))
                packed = jnp.where((lane8 == c * 2 + i // 8) & (sub8 == i % 8), one, packed)
        return packed

    pack_col[...] = pack_column(0)
    pack_own[...] = pack_column(COLS - 1)

    loads[0].wait()
    loads[2].wait()

    def sums(value, other):
        return (value * other).reshape(-1, 8, LANES).sum(axis=0)

    def plain(c, carry):
        cross, own = carry
        value = flat(body[c, 0:ROWS, 0:COLS, :])
        tail = flat(last[c, 0:ROWS, 0:COLS, :])
        acc_one[...] += self_product(value)
        return cross + sums(value, tail), own + sums(tail, tail)

    zero = jnp.zeros((8, LANES), F32)
    cross_one, own_one = lax.fori_loop(0, CHANNELS, plain, (zero, zero))

    pl.semaphore_wait(barrier, len(greeted))

    def remote(source, target, index, peer):
        return pltpu.make_async_remote_copy(
            source, target, halo_send.at[index], halo_recv.at[index], device_id=peer, device_id_type=MESH
        )

    lat_up = {"lat": lax.max(lat - 1, 0)}
    lat_down = {"lat": lax.min(lat + 1, n_lat - 1)}
    east_copies = [
        remote(fields.at[:, :, 0, main], east, 0, west_id),
        remote(pack_col, got_col, 1, west_id),
    ]
    south_copies = [
        remote(fields.at[:, 0, :, main], south, 2, lat_up),
        remote(pack_row, got_row, 3, lat_up),
    ]
    west_copy = remote(fields.at[:, :, COLS - 1, main], west, 4, east_id)
    north_copy = remote(fields.at[:, ROWS - 1, :, main], north, 5, lat_down)

    @pl.when(lat > 0)
    def _():
        for copy in south_copies:
            copy.start()

    for copy in east_copies:
        copy.start()

    @pl.when(lat < n_lat - 1)
    def _():
        north_copy.start()

    west_copy.start()

    def crossed(c, carry):
        cross, own = carry
        value = body[c, 0:ROWS, 0:COLS, :]
        tail = last[c, 0:ROWS, 0:COLS, :]
        lower = flat(value * body[c, 1 : ROWS + 1, 0:COLS, :])
        right = flat(value * body[c, 0:ROWS, 1 : COLS + 1, :])
        tail_lower = flat(tail * last[c, 1 : ROWS + 1, 0:COLS, :])
        tail_right = flat(tail * last[c, 0:ROWS, 1 : COLS + 1, :])
        acc_two[...] += self_product(lower)
        acc_two[...] += self_product(right)
        cross += sums(lower, tail_lower) + sums(right, tail_right)
        own += sums(tail_lower, tail_lower) + sums(tail_right, tail_right)
        return cross, own

    cross_two, own_two = lax.fori_loop(0, CHANNELS, crossed, (zero, zero))

    @pl.when(lat < n_lat - 1)
    def _():
        for copy in south_copies:
            copy.wait_recv()

    for copy in east_copies:
        copy.wait_recv()

    @pl.when(lat == n_lat - 1)
    def _():
        south[...] = jnp.zeros_like(south)
        got_row[...] = jnp.zeros_like(got_row)

    @pl.when(lat == 0)
    def _():
        north[...] = jnp.zeros_like(north)

    def spread(packed, lane):
        return jnp.broadcast_to(packed[:, lane : lane + 1], (8, LANES))

    row_packed, col_packed, own_packed = got_row[...], got_col[...], pack_own[...]
    tail_row = jnp.concatenate([spread(row_packed, lane) for lane in range(CHANNELS * 4)], axis=0)
    tail_row = tail_row * flat(last[:, ROWS - 1, 0:COLS, :])
    tail_col = [spread(col_packed, lane) * spread(own_packed, lane) for lane in range(CHANNELS * 2)]
    tails = jnp.concatenate([tail_row] + tail_col, axis=0)
    border = jnp.concatenate(
        [flat(body[:, ROWS - 1, 0:COLS, :] * south[...]), flat(edge[...] * east[...])], axis=0
    )
    acc_two[...] += self_product(border)
    cross_two += sums(border, tails)
    own_two += sums(tails, tails)

    total = acc_one[...] + 2.0 * acc_two[...]
    scale = 1.0 / cells_total
    full = (total[:LANES, :LANES] + total[LANES:, LANES:]) + (total[:LANES, LANES:] + total[LANES:, :LANES])
    full = full * scale
    cross = (cross_one + 2.0 * cross_two).sum(axis=0, keepdims=True) * scale
    own = (own_one + 2.0 * own_two).sum(axis=0, keepdims=True) * scale

    half = LANES // 2
    top, bottom = full[:half], full[half:]
    row, lane = iota((half, LANES), 0), iota((half, LANES), 1)
    folded = jnp.where((lane < half) & (row < lane), pltpu.roll(bottom, half, 1), top)
    diagonal = jnp.where(lane == row + half, bottom, 0.0).sum(axis=0, keepdims=True)
    extra = jnp.where(iota((1, LANES), 1) < half, own, diagonal)
    rows = half // n_lat
    for owner in range(n_lat):
        part[owner, 0:rows, :] = folded[owner * rows : (owner + 1) * rows]
        tail = cross if owner == 0 else extra if owner == 1 else jnp.zeros((1, LANES), F32)
        part[owner, rows : rows + 1, :] = tail

    def exchange(count, me, peer_of, device_of, source_of, buf, send, recv):
        copies = [
            pltpu.make_async_remote_copy(
                source_of(peer_of(step)), buf.at[me], send.at[step], recv.at[step],
                device_id=device_of(peer_of(step)), device_id_type=MESH,
            )
            for step in range(1, count)
        ]
        for copy in copies:
            copy.start()
        arrivals = [
            pltpu.make_async_remote_copy(
                buf.at[me], buf.at[peer_of(count - step)], send.at[step], recv.at[step],
                device_id=device_of(peer_of(step)), device_id_type=MESH,
            )
            for step in range(1, count)
        ]
        for copy in arrivals:
            copy.wait_recv()
        return copies

    def added(buf, count):
        result = buf[0]
        for index in range(1, count):
            result = result + buf[index]
        return result

    lat_buf[lat] = part[lat]
    pending = exchange(
        n_lat, lat, lat_peer, lambda p: {"lat": p}, lambda p: part.at[p], lat_buf, lat_send, lat_recv
    )
    y_buf[y] = added(lat_buf, n_lat)
    pending += exchange(
        n_y, y, y_peer, lambda p: {"lon": p * n_z + z}, lambda p: y_buf.at[y], y_buf, y_send, y_recv
    )
    z_buf[z] = added(y_buf, n_y)
    pending += exchange(
        n_z, z, z_peer, lambda p: {"lon": y * n_z + p}, lambda p: z_buf.at[z], z_buf, z_send, z_recv
    )
    all_buf[lat] = added(z_buf, n_z)
    pending += exchange(
        n_lat, lat, lat_peer, lambda p: {"lat": p}, lambda p: all_buf.at[lat], all_buf, all_send, all_recv
    )
    gram_out[...] = all_buf[...]

    @pl.when(lat > 0)
    def _():
        north_copy.wait_recv()
        for copy in south_copies:
            copy.wait_send()

    @pl.when(lat < n_lat - 1)
    def _():
        north_copy.wait_send()

    west_copy.wait_recv()
    for copy in [west_copy] + east_copies + pending:
        copy.wait_send()
    north_out[...] = north[...]
    south_out[...] = south[...]
    west_out[...] = west[...]
    east_out[...] = east[...]


def gram_call(fields, n_lat, n_lon):
    n_z = 8 if n_lon % 32 == 0 else max(n_lon // 2, 1)
    n_y = n_lon // n_z
    rows = LANES // 2 // n_lat + 1
    cells_total = 5 * CHANNELS * ROWS * n_lat * COLS * n_lon
    row_shape, col_shape = (CHANNELS, COLS, LANES), (CHANNELS, ROWS, LANES)
    chunk = (rows, LANES)
    dma = pltpu.SemaphoreType.DMA
    shapes = [(n_lat,) + chunk, row_shape, row_shape, col_shape, col_shape]
    vmem = pl.BlockSpec(memory_space=pltpu.VMEM)
    return pl.pallas_call(
        functools.partial(gram_kernel, (n_lat, n_y, n_z), cells_total),
        out_shape=[jax.ShapeDtypeStruct(shape, F32) for shape in shapes],
        in_specs=[pl.BlockSpec(memory_space=pl.ANY)],
        out_specs=[vmem] * 5,
        scratch_shapes=[
            pltpu.VMEM((CHANNELS, ROWS + 1, COLS + 8, LANES), F32),
            pltpu.VMEM((CHANNELS, ROWS, COLS, 1), F32),
            pltpu.VMEM((CHANNELS, ROWS + 1, COLS + 8, LANES), F32),
            pltpu.VMEM(col_shape, F32),
            pltpu.VMEM(row_shape, F32),
            pltpu.VMEM(row_shape, F32),
            pltpu.VMEM(col_shape, F32),
            pltpu.VMEM(col_shape, F32),
        ]
        + [pltpu.VMEM((8, LANES), F32)] * 5
        + [pltpu.VMEM((2 * LANES, 2 * LANES), F32)] * 2
        + [
            pltpu.VMEM((n_lat,) + chunk, F32),
            pltpu.VMEM((n_lat,) + chunk, F32),
            pltpu.VMEM((n_y,) + chunk, F32),
            pltpu.VMEM((n_z,) + chunk, F32),
            pltpu.VMEM((n_lat,) + chunk, F32),
            dma((3,)),
            dma((6,)), dma((6,)),
            dma((n_lat,)), dma((n_lat,)),
            dma((n_y,)), dma((n_y,)),
            dma((n_z,)), dma((n_z,)),
            dma((n_lat,)), dma((n_lat,)),
        ],
        compiler_params=pltpu.CompilerParams(
            collective_id=0, has_side_effects=True, vmem_limit_bytes=40 << 20
        ),
    )(fields)


def unfolded(gram):
    n_lat, rows, _ = gram.shape
    half = LANES // 2
    folded = jnp.concatenate([gram[owner, : rows - 1, :] for owner in range(n_lat)], axis=0)
    cross, extra = gram[0, rows - 1 : rows, :], gram[1, rows - 1 : rows, :]
    row, lane = iota((half, LANES), 0), iota((half, LANES), 1)
    top = jnp.where((lane < half) & (row <= lane), 0.0, folded)
    bottom = jnp.where((lane >= half) & (row < lane - half), pltpu.roll(folded, half, 1), 0.0)
    once = jnp.concatenate([top, bottom], axis=0)
    diagonal = jnp.concatenate(
        [jnp.where(lane == row, folded, 0.0), jnp.where(lane == row + half, jnp.broadcast_to(extra, (half, LANES)), 0.0)],
        axis=0,
    )
    full = once + once.T + diagonal
    row, lane = iota((LANES, LANES), 0), iota((LANES, LANES), 1)

    def column(line):
        return jnp.where(row == lane, jnp.broadcast_to(line, (LANES, LANES)), 0.0).sum(axis=1, keepdims=True)

    corner = extra[:, 0:1]
    shifted = pltpu.roll(pltpu.roll(full, LANES - 1, 0), LANES - 1, 1)
    line = jnp.where(iota((1, LANES), 1) == LANES - 1, corner, pltpu.roll(cross, LANES - 1, 1))
    shifted = jnp.where(lane == LANES - 1, column(line), shifted)
    shifted = jnp.where(row == LANES - 1, jnp.broadcast_to(line, (LANES, LANES)), shifted)
    identity = jnp.where(row == lane, 1.0, 0.0)
    first = jnp.where(lane == LANES - 1, column(cross), identity)
    low = jnp.where(row == LANES - 1, cross[:, 0:1], pltpu.roll(full, LANES - 1, 0)[:, 0:1])
    second = jnp.where(lane == LANES - 1, low, identity)
    return (full, first), (shifted, second)


def split_three(value):
    one = value.astype(BF16).astype(F32)
    two = (value - one).astype(BF16).astype(F32)
    return one, two, value - one - two


def eliminate(b, work, columns, first_row):
    start = b * 8
    sub, lane = iota((8, LANES), 0), iota((8, LANES), 1)
    block = pltpu.roll(work[b, :, 0:LANES], (LANES - start) % LANES, 1)
    for j in range(8):
        columns[j] = jnp.broadcast_to(block[:, j : j + 1], (8, LANES))
    entry = {}
    for i in range(8):
        for j in range(i, 8):
            entry[i, j] = jnp.broadcast_to(columns[j, i : i + 1, :], (8, LANES))
    left_rows = [jnp.broadcast_to(work[b, i : i + 1, 0:LANES], (8, LANES)) for i in range(8)]
    right_rows = [jnp.broadcast_to(work[b, i : i + 1, LANES : 2 * LANES], (8, LANES)) for i in range(8)]
    inverse = []
    for k in range(8):
        inverse.append(1.0 / entry[k, k])
        for i in range(k + 1, 8):
            factor = entry[k, i] * inverse[k]
            for j in range(i, 8):
                entry[i, j] = entry[i, j] - factor * entry[k, j]
            left_rows[i] = left_rows[i] - factor * left_rows[k]
            right_rows[i] = right_rows[i] - factor * right_rows[k]

    def gathered(rows):
        result = rows[0]
        for k in range(1, 8):
            result = jnp.where(sub == k, rows[k], result)
        return result

    pivots = gathered(inverse)
    done_left, done_right = gathered(left_rows), gathered(right_rows)
    f1, f2, f3 = split_three(jnp.where(lane >= start + 8, done_left * pivots, 0.0))
    d1, d2, d3 = split_three(jnp.concatenate([done_left, done_right], axis=1))
    factors = jnp.concatenate([f1, f1, f2, f1, f2, f3], axis=0).T.astype(BF16)
    done = jnp.concatenate([d1, d2, d1, d3, d2, d1], axis=0).astype(BF16)
    update = jnp.dot(factors[first_row:], done, preferred_element_type=F32)
    root = jnp.sqrt(pivots)
    work[b, :, 0:LANES] = done_left * root
    work[b, :, LANES : 2 * LANES] = done_right * root
    below = slice(first_row // 8, LANES // 8)
    work[below] = work[below] - update.reshape(-1, 8, 2 * LANES)


def accurate(left, right):
    return lax.dot_general(
        left, right, (((1,), (1,)), ((), ())), precision=lax.Precision.HIGHEST, preferred_element_type=F32
    )


def modes_kernel(
    fields, gram, north, south, west, east, modes, forward, backward,
    body, work_one, work_two, splat_one, splat_two, weights, plain, lower, left, right, load_sem, store_sem,
):
    works, splats = (work_one, work_two), (splat_one, splat_two)
    main = pl.ds(0, LANES)
    inner, across = pl.ds(1, ROWS), pl.ds(8, COLS)
    loads = [
        pltpu.make_async_copy(fields.at[:, :, :, main], body.at[:, inner, across, :], load_sem.at[0]),
        pltpu.make_async_copy(north, body.at[:, 0, across, :], load_sem.at[1]),
        pltpu.make_async_copy(south, body.at[:, ROWS + 1, across, :], load_sem.at[2]),
        pltpu.make_async_copy(west, body.at[:, inner, 7, :], load_sem.at[3]),
        pltpu.make_async_copy(east, body.at[:, inner, 8 + COLS, :], load_sem.at[4]),
    ]
    for copy in loads:
        copy.start()

    for work, (matrix, extended) in zip(works, unfolded(gram[...])):
        work[:, :, 0:LANES] = matrix.reshape(-1, 8, LANES)
        work[:, :, LANES : 2 * LANES] = extended.reshape(-1, 8, LANES)

    for phase in range(4):

        def step(b, carry):
            for work, columns in zip(works, splats):
                eliminate(b, work, columns, phase * 32)
            return carry

        lax.fori_loop(phase * 4, phase * 4 + 4, step, 0)

    row, lane = iota((LANES, LANES), 0), iota((LANES, LANES), 1)

    def parts(c):
        factor, extended = flat(works[c][:, :, 0:LANES]), flat(works[c][:, :, LANES : 2 * LANES])
        corner = jnp.where((row == LANES - 1) & (lane == LANES - 1), 1.0 / factor, 0.0)
        return factor, extended, jnp.where(lane == LANES - 1, corner, extended)

    factor, extended, inverse = parts(0)
    mixing = inverse.T
    high = mixing.astype(BF16)
    low = (mixing - high.astype(F32)).astype(BF16)
    line = jnp.concatenate([high, low], axis=1)
    weights[...] = jnp.concatenate([line, line], axis=0)

    for copy in loads:
        copy.wait()

    def mixed(value):
        both = jnp.dot(split_pair(value), weights[...], preferred_element_type=F32)
        return both[:, :LANES] + both[:, LANES:]

    def stores(c):
        return [
            pltpu.make_async_copy(plain.at[c], modes.at[c], store_sem.at[0, c]),
            pltpu.make_async_copy(lower.at[c, pl.ds(0, ROWS)], modes.at[CHANNELS + c], store_sem.at[1, c]),
            pltpu.make_async_copy(lower.at[c, pl.ds(1, ROWS)], modes.at[2 * CHANNELS + c], store_sem.at[2, c]),
            pltpu.make_async_copy(left.at[c], modes.at[3 * CHANNELS + c], store_sem.at[3, c]),
            pltpu.make_async_copy(right.at[c], modes.at[4 * CHANNELS + c], store_sem.at[4, c]),
        ]

    def channel(c, carry):
        value = body[c, 1 : ROWS + 1, 8 : 8 + COLS, :]
        shape = (ROWS, COLS, LANES)
        plain[c] = mixed(flat(value)).reshape(shape)
        pairs = body[c, 0 : ROWS + 1, 8 : 8 + COLS, :] * body[c, 1 : ROWS + 2, 8 : 8 + COLS, :]
        lower[c] = mixed(flat(pairs)).reshape((ROWS + 1, COLS, LANES))
        left[c] = mixed(flat(value * body[c, 1 : ROWS + 1, 7 : 7 + COLS, :])).reshape(shape)
        right[c] = mixed(flat(value * body[c, 1 : ROWS + 1, 9 : 9 + COLS, :])).reshape(shape)
        for copy in stores(c):
            copy.start()
        return carry

    lax.fori_loop(0, CHANNELS, channel, 0)

    shifted = jnp.where(lane == LANES - 1, extended, pltpu.roll(factor, LANES - 1, 1))
    forward[...] = accurate(shifted, inverse)
    factor, extended, inverse = parts(1)
    mixed_block = jnp.where(lane == 0, pltpu.roll(extended, 1, 1), pltpu.roll(factor, 1, 1))
    backward[...] = accurate(mixed_block, inverse)

    def finish(c, carry):
        for copy in stores(c):
            copy.wait()
        return carry

    lax.fori_loop(0, CHANNELS, finish, 0)


def modes_call(fields, gram, north, south, west, east):
    shape = (CHANNELS, ROWS, COLS, LANES)
    any_space = pl.BlockSpec(memory_space=pl.ANY)
    vmem = pl.BlockSpec(memory_space=pltpu.VMEM)
    return pl.pallas_call(
        modes_kernel,
        out_shape=[
            jax.ShapeDtypeStruct((5 * CHANNELS, ROWS, COLS, LANES), F32),
            jax.ShapeDtypeStruct((LANES, LANES), F32),
            jax.ShapeDtypeStruct((LANES, LANES), F32),
        ],
        in_specs=[any_space, vmem, any_space, any_space, any_space, any_space],
        out_specs=[any_space, vmem, vmem],
        scratch_shapes=[
            pltpu.VMEM((CHANNELS, ROWS + 2, COLS + 16, LANES), F32),
            pltpu.VMEM((LANES // 8, 8, 2 * LANES), F32),
            pltpu.VMEM((LANES // 8, 8, 2 * LANES), F32),
            pltpu.VMEM((8, 8, LANES), F32),
            pltpu.VMEM((8, 8, LANES), F32),
            pltpu.VMEM((2 * LANES, 2 * LANES), BF16),
            pltpu.VMEM(shape, F32),
            pltpu.VMEM((CHANNELS, ROWS + 1, COLS, LANES), F32),
            pltpu.VMEM(shape, F32),
            pltpu.VMEM(shape, F32),
            pltpu.SemaphoreType.DMA((5,)),
            pltpu.SemaphoreType.DMA((5, CHANNELS)),
        ],
        compiler_params=pltpu.CompilerParams(vmem_limit_bytes=40 << 20),
    )(fields, gram, north, south, west, east)


def shards(fields):
    cells = fields.transpose(1, 2, 3, 0)
    gram, north, south, west, east = gram_call(cells, lax.axis_size("lat"), lax.axis_size("lon"))
    return tuple(modes_call(cells, gram, north, south, west, east))


def solution(mesh):
    return jax.shard_map(
        shards,
        mesh=mesh,
        in_specs=(P(None, None, "lat", "lon"),),
        out_specs=(P(None, "lat", "lon", None), P(), P()),
        check_vma=False,
    )
```

```python
import functools

import jax
import jax.numpy as jnp
from jax import lax
from jax.experimental import pallas as pl
from jax.experimental.pallas import tpu as pltpu
from jax.sharding import PartitionSpec as P

F32, BF16 = jnp.float32, jnp.bfloat16
MESH = pl.DeviceIdType.MESH
CHANNELS, ROWS, COLS, LANES = 6, 16, 32, 128


def split_pair(value):
    high = value.astype(BF16)
    low = (value - high.astype(F32)).astype(BF16)
    return jnp.concatenate([high, low], axis=-1)


def flat(value):
    return value.reshape(-1, value.shape[-1])


def iota(shape, dim):
    return lax.broadcasted_iota(jnp.int32, shape, dim)


def sums(value, other):
    return (value * other).reshape(-1, 8, LANES).sum(axis=0)


def self_product(value, tails=None):
    high = value.astype(BF16)
    rest = value - high.astype(F32)
    pair = jnp.concatenate([high, rest.astype(BF16)], axis=-1)
    turned = high.T
    if tails is not None:
        turned = jnp.concatenate([turned, tails], axis=0)
    return jnp.dot(turned, pair, preferred_element_type=F32), sums(rest, rest)


def gram_kernel(
    sizes, cells_total, fields,
    gram_out, north_out, south_out, west_out, east_out,
    body, last, edge, north, south, west, east,
    pack_row, pack_col, got_row, got_col, tail_cells, tails_ref,
    acc_one, acc_two, part, lat_buf, y_buf, z_buf, all_buf,
    load_sem, tail_sem, halo_send, halo_recv, lat_send, lat_recv, y_send, y_recv, z_send, z_recv, all_send, all_recv,
):
    n_lat, n_y, n_z = sizes
    n_lon = n_y * n_z
    lat, lon = lax.axis_index("lat"), lax.axis_index("lon")
    y, z = lon // n_z, lon % n_z
    above, below = lon - 1 + n_lon, lon + 1
    west_id, east_id = {"lon": above % n_lon}, {"lon": below % n_lon}

    def lat_peer(step):
        return (lat + step) % n_lat

    def y_peer(step):
        return (y + step) % n_y

    def z_peer(step):
        return (z + step) % n_z

    barrier = pltpu.get_barrier_semaphore()
    greeted = [west_id, east_id]
    greeted += [{"lat": lat_peer(step)} for step in range(1, n_lat)]
    greeted += [{"lon": y_peer(step) * n_z + z} for step in range(1, n_y)]
    greeted += [{"lon": y * n_z + z_peer(step)} for step in range(1, n_z)]
    for peer in greeted:
        pl.semaphore_signal(barrier, inc=1, device_id=peer, device_id_type=MESH)

    main = pl.ds(0, LANES)

    def load(c):
        return pltpu.make_async_copy(
            fields.at[c, :, :, main], body.at[c, pl.ds(0, ROWS), pl.ds(0, COLS), :], load_sem.at[c]
        )

    tail_load = pltpu.make_async_copy(
        fields.at[:, :, :, pl.ds(LANES, 1)], last, tail_sem.at[0]
    )
    edge_load = pltpu.make_async_copy(fields.at[:, :, COLS - 1, main], edge, tail_sem.at[1])
    tail_load.start()

    def start_load(c, carry):
        load(c).start()
        return carry

    lax.fori_loop(0, CHANNELS, start_load, 0)
    edge_load.start()

    pl.semaphore_wait(barrier, len(greeted))
    def remote(source, target, index, peer):
        return pltpu.make_async_remote_copy(
            source, target, halo_send.at[index], halo_recv.at[index], device_id=peer, device_id_type=MESH
        )

    lat_up = {"lat": lax.max(lat - 1, 0)}
    lat_down = {"lat": lax.min(lat + 1, n_lat - 1)}
    east_copies = [
        remote(fields.at[:, :, 0, main], east, 0, west_id),
        remote(pack_col, got_col, 1, west_id),
    ]
    south_copies = [
        remote(fields.at[:, 0, :, main], south, 2, lat_up),
        remote(pack_row, got_row, 3, lat_up),
    ]
    west_copy = remote(fields.at[:, :, COLS - 1, main], west, 4, east_id)
    north_copy = remote(fields.at[:, ROWS - 1, :, main], north, 5, lat_down)

    @pl.when(lat > 0)
    def _():
        south_copies[0].start()

    east_copies[0].start()

    @pl.when(lat < n_lat - 1)
    def _():
        north_copy.start()

    west_copy.start()

    body[:, ROWS : ROWS + 1, 0:COLS, :] = jnp.zeros((CHANNELS, 1, COLS, LANES), F32)
    body[:, :, COLS : COLS + 8, :] = jnp.zeros((CHANNELS, ROWS + 1, 8, LANES), F32)
    acc_one[...] = jnp.zeros_like(acc_one)
    acc_two[...] = jnp.zeros_like(acc_two)

    tail_load.wait()
    wide_lane = iota((LANES, LANES), 1)
    merged = jnp.zeros((LANES, LANES), F32)
    for c in range(CHANNELS):
        for q in range(4):
            line = last[c, 4 * q : 4 * q + 4].reshape(LANES, 1)
            merged = jnp.where(wide_lane == 4 * c + q, jnp.broadcast_to(line, (LANES, LANES)), merged)
    tail_cells[...] = merged
    pack_row[...] = merged[0:COLS]
    sub8 = iota((8, LANES), 0)

    def column(ref_or_value, j):
        lines = [jnp.broadcast_to(ref_or_value[COLS * i + j : COLS * i + j + 1, :], (8, LANES)) for i in range(4)]
        result = lines[3]
        for i in range(3):
            result = jnp.where(sub8 == i, lines[i], result)
        return result

    pack_col[...] = column(tail_cells, 0)
    east_copies[1].start()

    @pl.when(lat > 0)
    def _():
        south_copies[1].start()

    count = 4 * CHANNELS
    tail = merged.T[:count]
    row, lane = iota((count, LANES), 0), iota((count, LANES), 1)
    right = tail * jnp.where(lane % COLS == COLS - 1, 0.0, pltpu.roll(tail, LANES - 1, 1))
    ahead = pltpu.roll(tail, LANES - COLS, 1)
    further = jnp.where(row % 4 == 3, 0.0, pltpu.roll(ahead, count - 1, 0))
    lower = tail * jnp.where(lane < LANES - COLS, ahead, further)
    for f, values in enumerate((tail, lower, right)):
        high = values.astype(BF16).astype(F32)
        low = values - high
        for pair in range(CHANNELS // 2):
            high8, low8 = high[8 * pair : 8 * pair + 8], low[8 * pair : 8 * pair + 8]
            first = jnp.where(sub8 < 4, high8, pltpu.roll(low8, 4, 0))
            second = jnp.where(sub8 < 4, pltpu.roll(high8, 4, 0), low8)
            for c, both in ((2 * pair, first), (2 * pair + 1, second)):
                for q in range(4):
                    part_q = jnp.where(sub8 % 4 == q, both, 0.0)
                    part_q = jnp.concatenate([part_q, jnp.zeros((8, LANES), F32)], axis=0)
                    tails_ref[f, c, :, LANES * q : LANES * q + LANES] = part_q.astype(BF16)
    own_one = sums(tail, tail)
    own_two = sums(lower, lower) + sums(right, right)

    zero = jnp.zeros((8, LANES), F32)

    def channel(c, carry):
        rest_one, rest_two = carry
        load(c).wait()
        value = body[c, 0:ROWS, 0:COLS, :]
        product, rest = self_product(flat(value), tails_ref[0, c])
        acc_one[...] += product
        rest_one += rest
        product, rest = self_product(flat(value * body[c, 1 : ROWS + 1, 0:COLS, :]), tails_ref[1, c])
        acc_two[...] += product
        rest_two += rest
        product, rest = self_product(flat(value * body[c, 0:ROWS, 1 : COLS + 1, :]), tails_ref[2, c])
        acc_two[...] += product
        rest_two += rest
        return rest_one, rest_two

    rest_one, rest_two = lax.fori_loop(0, CHANNELS, channel, (zero, zero))
    edge_load.wait()

    @pl.when(lat < n_lat - 1)
    def _():
        for copy in south_copies:
            copy.wait_recv()

    for copy in east_copies:
        copy.wait_recv()

    @pl.when(lat == n_lat - 1)
    def _():
        south[...] = jnp.zeros_like(south)
        got_row[...] = jnp.zeros_like(got_row)

    @pl.when(lat == 0)
    def _():
        north[...] = jnp.zeros_like(north)

    def spread(packed, lane):
        return jnp.broadcast_to(packed[:, lane : lane + 1], (8, LANES))

    row_pairs = pltpu.roll(tail_cells[LANES - COLS : LANES, :], LANES - 3, 1) * got_row[...]
    column_pairs = column(tail_cells, COLS - 1) * got_col[...]
    column_pairs = jnp.where(sub8 < 4, column_pairs, pltpu.roll(pltpu.roll(column_pairs, 4, 0), LANES - 1, 1))
    tails = [
        spread(row_pairs[8 * t : 8 * t + 8], 4 * c) for c in range(CHANNELS) for t in range(COLS // 8)
    ]
    tails += [spread(column_pairs, 4 * c + 2 * h) for c in range(CHANNELS) for h in range(2)]
    tails = jnp.concatenate(tails, axis=0)
    border = jnp.concatenate(
        [flat(body[:, ROWS - 1, 0:COLS, :] * south[...]), flat(edge[...] * east[...])], axis=0
    )
    product, rest = self_product(border)
    rest_two += rest
    cross_two = sums(border, tails)
    border_own = sums(tails, tails).sum(axis=0, keepdims=True)

    scale = 1.0 / cells_total
    total = (acc_one[...] + 2.0 * acc_two[...]) * scale
    rest = (rest_one + 2.0 * rest_two).sum(axis=0, keepdims=True) * scale
    square = total[:LANES] + product * (2.0 * scale)
    twisted = square[:, LANES:]
    full = square[:, :LANES] + (twisted + twisted.T)
    full += jnp.where(iota((LANES, LANES), 0) == iota((LANES, LANES), 1), rest, 0.0)
    cross = cross_two.sum(axis=0, keepdims=True) * (2.0 * scale)
    mixed = total[LANES : LANES + 8]
    mixed = mixed[:, :LANES] + jnp.where(sub8 < 4, mixed[:, LANES:], 0.0)
    cross += mixed.sum(axis=0, keepdims=True)
    own = (own_one + 2.0 * own_two).sum(axis=0, keepdims=True).sum(axis=1, keepdims=True)
    own = (jnp.broadcast_to(own, (1, LANES)) + 2.0 * border_own) * scale

    half = LANES // 2
    top, bottom = full[:half], full[half:]
    row, lane = iota((half, LANES), 0), iota((half, LANES), 1)
    folded = jnp.where((lane < half) & (row < lane), pltpu.roll(bottom, half, 1), top)
    diagonal = jnp.where(lane == row + half, bottom, 0.0).sum(axis=0, keepdims=True)
    extra = jnp.where(iota((1, LANES), 1) < half, own, diagonal)
    rows = half // n_lat
    for owner in range(n_lat):
        part[owner, 0:rows, :] = folded[owner * rows : (owner + 1) * rows]
        tail = cross if owner == 0 else extra if owner == 1 else jnp.zeros((1, LANES), F32)
        part[owner, rows : rows + 1, :] = tail

    def exchange(count, me, peer_of, device_of, source_of, buf, send, recv):
        def start(step, carry):
            peer = peer_of(step)
            pltpu.make_async_remote_copy(
                source_of(peer), buf.at[me], send.at[0], recv.at[0], device_id=device_of(peer), device_id_type=MESH
            ).start()
            return carry

        lax.fori_loop(1, count, start, 0)
        others = buf.at[pl.ds(0, count - 1)]
        pltpu.make_async_copy(others, others, recv.at[0]).wait()
        return pltpu.make_async_copy(others, others, send.at[0])

    def added(buf, count):
        result = buf[0]
        for index in range(1, count):
            result = result + buf[index]
        return result

    lat_buf[lat] = part[lat]
    pending = [exchange(
        n_lat, lat, lat_peer, lambda p: {"lat": p}, lambda p: part.at[p], lat_buf, lat_send, lat_recv
    )]
    y_buf[y] = added(lat_buf, n_lat)
    pending += [exchange(
        n_y, y, y_peer, lambda p: {"lon": p * n_z + z}, lambda p: y_buf.at[y], y_buf, y_send, y_recv
    )]
    z_buf[z] = added(y_buf, n_y)
    pending += [exchange(
        n_z, z, z_peer, lambda p: {"lon": y * n_z + p}, lambda p: z_buf.at[z], z_buf, z_send, z_recv
    )]
    all_buf[lat] = added(z_buf, n_z)
    pending += [exchange(
        n_lat, lat, lat_peer, lambda p: {"lat": p}, lambda p: all_buf.at[lat], all_buf, all_send, all_recv
    )]
    gram_out[...] = all_buf[...]

    @pl.when(lat > 0)
    def _():
        north_copy.wait_recv()
        for copy in south_copies:
            copy.wait_send()

    @pl.when(lat < n_lat - 1)
    def _():
        north_copy.wait_send()

    west_copy.wait_recv()
    for copy in [west_copy] + east_copies:
        copy.wait_send()
    for copy in pending:
        copy.wait()
    north_out[...] = north[...]
    south_out[...] = south[...]
    west_out[...] = west[...]
    east_out[...] = east[...]


def gram_call(fields, n_lat, n_lon):
    n_z = 8 if n_lon % 32 == 0 else max(n_lon // 2, 1)
    n_y = n_lon // n_z
    rows = LANES // 2 // n_lat + 1
    cells_total = 5 * CHANNELS * ROWS * n_lat * COLS * n_lon
    row_shape, col_shape = (CHANNELS, COLS, LANES), (CHANNELS, ROWS, LANES)
    chunk = (rows, LANES)
    dma = pltpu.SemaphoreType.DMA
    shapes = [(n_lat,) + chunk, row_shape, row_shape, col_shape, col_shape]
    vmem = pl.BlockSpec(memory_space=pltpu.VMEM)
    return pl.pallas_call(
        functools.partial(gram_kernel, (n_lat, n_y, n_z), cells_total),
        out_shape=[jax.ShapeDtypeStruct(shape, F32) for shape in shapes],
        in_specs=[pl.BlockSpec(memory_space=pltpu.HBM)],
        out_specs=[vmem] * 5,
        scratch_shapes=[
            pltpu.VMEM((CHANNELS, ROWS + 1, COLS + 8, LANES), F32),
            pltpu.VMEM((CHANNELS, ROWS, COLS, 1), F32),
            pltpu.VMEM(col_shape, F32),
            pltpu.VMEM(row_shape, F32),
            pltpu.VMEM(row_shape, F32),
            pltpu.VMEM(col_shape, F32),
            pltpu.VMEM(col_shape, F32),
        ]
        + [pltpu.VMEM((COLS, LANES), F32), pltpu.VMEM((8, LANES), F32)] * 2
        + [pltpu.VMEM((LANES, LANES), F32), pltpu.VMEM((3, CHANNELS, 16, 4 * LANES), BF16)]
        + [pltpu.VMEM((LANES + 16, 2 * LANES), F32)] * 2
        + [
            pltpu.VMEM((n_lat,) + chunk, F32),
            pltpu.VMEM((n_lat,) + chunk, F32),
            pltpu.VMEM((n_y,) + chunk, F32),
            pltpu.VMEM((n_z,) + chunk, F32),
            pltpu.VMEM((n_lat,) + chunk, F32),
            dma((CHANNELS,)), dma((2,)),
            dma((6,)), dma((6,)),
            dma((1,)), dma((1,)),
            dma((1,)), dma((1,)),
            dma((1,)), dma((1,)),
            dma((1,)), dma((1,)),
        ],
        compiler_params=pltpu.CompilerParams(
            collective_id=0, has_side_effects=True, vmem_limit_bytes=64_500_000
        ),
    )(fields)


def unfolded(gram):
    n_lat, rows, _ = gram.shape
    half = LANES // 2
    folded = jnp.concatenate([gram[owner, : rows - 1, :] for owner in range(n_lat)], axis=0)
    cross, extra = gram[0, rows - 1 : rows, :], gram[1, rows - 1 : rows, :]
    row, lane = iota((half, LANES), 0), iota((half, LANES), 1)
    top = jnp.where((lane < half) & (row <= lane), 0.0, folded)
    bottom = jnp.where((lane >= half) & (row < lane - half), pltpu.roll(folded, half, 1), 0.0)
    once = jnp.concatenate([top, bottom], axis=0)
    diagonal = jnp.concatenate(
        [jnp.where(lane == row, folded, 0.0), jnp.where(lane == row + half, jnp.broadcast_to(extra, (half, LANES)), 0.0)],
        axis=0,
    )
    full = once + once.T + diagonal
    row, lane = iota((LANES, LANES), 0), iota((LANES, LANES), 1)

    def column(line):
        return jnp.where(row == lane, jnp.broadcast_to(line, (LANES, LANES)), 0.0).sum(axis=1, keepdims=True)

    corner = extra[:, 0:1]
    shifted = pltpu.roll(pltpu.roll(full, LANES - 1, 0), LANES - 1, 1)
    line = jnp.where(iota((1, LANES), 1) == LANES - 1, corner, pltpu.roll(cross, LANES - 1, 1))
    shifted = jnp.where(lane == LANES - 1, column(line), shifted)
    shifted = jnp.where(row == LANES - 1, jnp.broadcast_to(line, (LANES, LANES)), shifted)
    identity = jnp.where(row == lane, 1.0, 0.0)
    first = jnp.where(lane == LANES - 1, column(cross), identity)
    low = jnp.where(row == LANES - 1, cross[:, 0:1], pltpu.roll(full, LANES - 1, 0)[:, 0:1])
    second = jnp.where(lane == LANES - 1, low, identity)
    return (full, first), (shifted, second)


def split_three(value):
    one = value.astype(BF16).astype(F32)
    two = (value - one).astype(BF16).astype(F32)
    return one, two, value - one - two


def eliminate(b, work, columns, first_row):
    start = b * 8
    sub, lane = iota((8, LANES), 0), iota((8, LANES), 1)
    block = pltpu.roll(work[b, :, 0:LANES], (LANES - start) % LANES, 1)
    for j in range(8):
        columns[j] = jnp.broadcast_to(block[:, j : j + 1], (8, LANES))
    entry = {}
    for i in range(8):
        for j in range(i, 8):
            entry[i, j] = jnp.broadcast_to(columns[j, i : i + 1, :], (8, LANES))
    left_rows = [jnp.broadcast_to(work[b, i : i + 1, 0:LANES], (8, LANES)) for i in range(8)]
    right_rows = [jnp.broadcast_to(work[b, i : i + 1, LANES : 2 * LANES], (8, LANES)) for i in range(8)]
    inverse = []
    for k in range(8):
        inverse.append(1.0 / entry[k, k])
        for i in range(k + 1, 8):
            factor = entry[k, i] * inverse[k]
            for j in range(i, 8):
                entry[i, j] = entry[i, j] - factor * entry[k, j]
            left_rows[i] = left_rows[i] - factor * left_rows[k]
            right_rows[i] = right_rows[i] - factor * right_rows[k]

    def gathered(rows):
        result = rows[0]
        for k in range(1, 8):
            result = jnp.where(sub == k, rows[k], result)
        return result

    pivots = gathered(inverse)
    done_left, done_right = gathered(left_rows), gathered(right_rows)
    f1, f2, f3 = split_three(jnp.where(lane >= start + 8, done_left * pivots, 0.0))
    d1, d2, d3 = split_three(jnp.concatenate([done_left, done_right], axis=1))
    factors = jnp.concatenate([f1, f1, f2, f1, f2, f3], axis=0).T.astype(BF16)
    done = jnp.concatenate([d1, d2, d1, d3, d2, d1], axis=0).astype(BF16)
    update = jnp.dot(factors[first_row:], done, preferred_element_type=F32)
    root = jnp.sqrt(pivots)
    work[b, :, 0:LANES] = done_left * root
    work[b, :, LANES : 2 * LANES] = done_right * root
    below = slice(first_row // 8, LANES // 8)
    work[below] = work[below] - update.reshape(-1, 8, 2 * LANES)


def accurate(left, right):
    return lax.dot_general(
        left, right, (((1,), (1,)), ((), ())), precision=lax.Precision.HIGHEST, preferred_element_type=F32
    )


def modes_kernel(
    fields, gram, north, south, west, east, modes, forward, backward,
    body, work_one, work_two, splat_one, splat_two, weights, plain, lower, left, right, load_sem, store_sem,
):
    works, splats = (work_one, work_two), (splat_one, splat_two)
    main = pl.ds(0, LANES)
    inner, across = pl.ds(1, ROWS), pl.ds(8, COLS)
    loads = [
        pltpu.make_async_copy(fields.at[:, :, :, main], body.at[:, inner, across, :], load_sem.at[0]),
        pltpu.make_async_copy(north, body.at[:, 0, across, :], load_sem.at[1]),
        pltpu.make_async_copy(south, body.at[:, ROWS + 1, across, :], load_sem.at[2]),
        pltpu.make_async_copy(west, body.at[:, inner, 7, :], load_sem.at[3]),
        pltpu.make_async_copy(east, body.at[:, inner, 8 + COLS, :], load_sem.at[4]),
    ]
    for copy in loads:
        copy.start()

    for work, (matrix, extended) in zip(works, unfolded(gram[...])):
        work[:, :, 0:LANES] = matrix.reshape(-1, 8, LANES)
        work[:, :, LANES : 2 * LANES] = extended.reshape(-1, 8, LANES)

    for phase in range(4):

        def step(b, carry):
            for work, columns in zip(works, splats):
                eliminate(b, work, columns, phase * 32)
            return carry

        lax.fori_loop(phase * 4, phase * 4 + 4, step, 0)

    row, lane = iota((LANES, LANES), 0), iota((LANES, LANES), 1)

    def parts(c):
        factor, extended = flat(works[c][:, :, 0:LANES]), flat(works[c][:, :, LANES : 2 * LANES])
        corner = jnp.where((row == LANES - 1) & (lane == LANES - 1), 1.0 / factor, 0.0)
        return factor, extended, jnp.where(lane == LANES - 1, corner, extended)

    factor, extended, inverse = parts(0)
    mixing = inverse.T
    high = mixing.astype(BF16)
    low = (mixing - high.astype(F32)).astype(BF16)
    line = jnp.concatenate([high, low], axis=1)
    weights[...] = jnp.concatenate([line, line], axis=0)

    for copy in loads:
        copy.wait()

    def mixed(value):
        both = jnp.dot(split_pair(value), weights[...], preferred_element_type=F32)
        return both[:, :LANES] + both[:, LANES:]

    def stores(c):
        return [
            pltpu.make_async_copy(plain.at[c], modes.at[c], store_sem.at[0, c]),
            pltpu.make_async_copy(lower.at[c, pl.ds(0, ROWS)], modes.at[CHANNELS + c], store_sem.at[1, c]),
            pltpu.make_async_copy(lower.at[c, pl.ds(1, ROWS)], modes.at[2 * CHANNELS + c], store_sem.at[2, c]),
            pltpu.make_async_copy(left.at[c], modes.at[3 * CHANNELS + c], store_sem.at[3, c]),
            pltpu.make_async_copy(right.at[c], modes.at[4 * CHANNELS + c], store_sem.at[4, c]),
        ]

    def channel(c, carry):
        value = body[c, 1 : ROWS + 1, 8 : 8 + COLS, :]
        shape = (ROWS, COLS, LANES)
        plain[c] = mixed(flat(value)).reshape(shape)
        pairs = body[c, 0 : ROWS + 1, 8 : 8 + COLS, :] * body[c, 1 : ROWS + 2, 8 : 8 + COLS, :]
        lower[c] = mixed(flat(pairs)).reshape((ROWS + 1, COLS, LANES))
        left[c] = mixed(flat(value * body[c, 1 : ROWS + 1, 7 : 7 + COLS, :])).reshape(shape)
        right[c] = mixed(flat(value * body[c, 1 : ROWS + 1, 9 : 9 + COLS, :])).reshape(shape)
        for copy in stores(c):
            copy.start()
        return carry

    lax.fori_loop(0, CHANNELS, channel, 0)

    shifted = jnp.where(lane == LANES - 1, extended, pltpu.roll(factor, LANES - 1, 1))
    forward[...] = accurate(shifted, inverse)
    factor, extended, inverse = parts(1)
    mixed_block = jnp.where(lane == 0, pltpu.roll(extended, 1, 1), pltpu.roll(factor, 1, 1))
    backward[...] = accurate(mixed_block, inverse)

    def finish(c, carry):
        for copy in stores(c):
            copy.wait()
        return carry

    lax.fori_loop(0, CHANNELS, finish, 0)


def modes_call(fields, gram, north, south, west, east):
    shape = (CHANNELS, ROWS, COLS, LANES)
    any_space = pl.BlockSpec(memory_space=pl.ANY)
    vmem = pl.BlockSpec(memory_space=pltpu.VMEM)
    return pl.pallas_call(
        modes_kernel,
        out_shape=[
            jax.ShapeDtypeStruct((5 * CHANNELS, ROWS, COLS, LANES), F32),
            jax.ShapeDtypeStruct((LANES, LANES), F32),
            jax.ShapeDtypeStruct((LANES, LANES), F32),
        ],
        in_specs=[pl.BlockSpec(memory_space=pltpu.HBM), vmem, any_space, any_space, any_space, any_space],
        out_specs=[any_space, vmem, vmem],
        scratch_shapes=[
            pltpu.VMEM((CHANNELS, ROWS + 2, COLS + 16, LANES), F32),
            pltpu.VMEM((LANES // 8, 8, 2 * LANES), F32),
            pltpu.VMEM((LANES // 8, 8, 2 * LANES), F32),
            pltpu.VMEM((8, 8, LANES), F32),
            pltpu.VMEM((8, 8, LANES), F32),
            pltpu.VMEM((2 * LANES, 2 * LANES), BF16),
            pltpu.VMEM(shape, F32),
            pltpu.VMEM((CHANNELS, ROWS + 1, COLS, LANES), F32),
            pltpu.VMEM(shape, F32),
            pltpu.VMEM(shape, F32),
            pltpu.SemaphoreType.DMA((5,)),
            pltpu.SemaphoreType.DMA((5, CHANNELS)),
        ],
        compiler_params=pltpu.CompilerParams(vmem_limit_bytes=64_500_000),
    )(fields, gram, north, south, west, east)


def shards(fields):
    cells = fields.transpose(1, 2, 3, 0)
    gram, north, south, west, east = gram_call(cells, lax.axis_size("lat"), lax.axis_size("lon"))
    return tuple(modes_call(cells, gram, north, south, west, east))


def solution(mesh):
    return jax.shard_map(
        shards,
        mesh=mesh,
        in_specs=(P(None, None, "lat", "lon"),),
        out_specs=(P(None, "lat", "lon", None), P(), P()),
        check_vma=False,
    )
```

```python
import functools

import jax
import jax.numpy as jnp
from jax import lax
from jax.experimental import pallas as pl
from jax.experimental.pallas import tpu as pltpu
from jax.sharding import PartitionSpec as P

F32, BF16 = jnp.float32, jnp.bfloat16
MESH = pl.DeviceIdType.MESH
CHANNELS, ROWS, COLS, LANES = 6, 16, 32, 128


def split_pair(value):
    high = value.astype(BF16)
    low = (value - high.astype(F32)).astype(BF16)
    return jnp.concatenate([high, low], axis=-1)


def flat(value):
    return value.reshape(-1, value.shape[-1])


def iota(shape, dim):
    return lax.broadcasted_iota(jnp.int32, shape, dim)


def sums(value, other):
    return (value * other).reshape(-1, 8, LANES).sum(axis=0)


def self_product(value, tails=None):
    high = value.astype(BF16)
    rest = value - high.astype(F32)
    pair = jnp.concatenate([high, rest.astype(BF16)], axis=-1)
    turned = high.T
    if tails is not None:
        turned = jnp.concatenate([turned, tails], axis=0)
    return jnp.dot(turned, pair, preferred_element_type=F32), sums(rest, rest)


def gram_kernel(
    sizes, cells_total, fields,
    gram_out, north_out, south_out, west_out, east_out,
    body, last, edge, north, south, west, east,
    pack_row, pack_col, got_row, got_col, tail_cells, tails_ref,
    acc_one, acc_two, part, lat_buf, y_buf, z_buf, all_buf,
    load_sem, tail_sem, halo_send, halo_recv, lat_send, lat_recv, y_send, y_recv, z_send, z_recv, all_send, all_recv,
):
    n_lat, n_y, n_z = sizes
    n_lon = n_y * n_z
    lat, lon = lax.axis_index("lat"), lax.axis_index("lon")
    y, z = lon // n_z, lon % n_z
    above, below = lon - 1 + n_lon, lon + 1
    west_id, east_id = {"lon": above % n_lon}, {"lon": below % n_lon}

    def lat_peer(step):
        return (lat + step) % n_lat

    def y_peer(step):
        return (y + step) % n_y

    def z_peer(step):
        return (z + step) % n_z

    barrier = pltpu.get_barrier_semaphore()
    greeted = [west_id, east_id]
    greeted += [{"lat": lat_peer(step)} for step in range(1, n_lat)]
    greeted += [{"lon": y_peer(step) * n_z + z} for step in range(1, n_y)]
    greeted += [{"lon": y * n_z + z_peer(step)} for step in range(1, n_z)]
    for peer in greeted:
        pl.semaphore_signal(barrier, inc=1, device_id=peer, device_id_type=MESH)

    main = pl.ds(0, LANES)

    def load(c):
        return pltpu.make_async_copy(
            fields.at[c, :, :, main], body.at[c, pl.ds(0, ROWS), pl.ds(0, COLS), :], load_sem.at[c]
        )

    tail_load = pltpu.make_async_copy(
        fields.at[:, :, :, pl.ds(LANES, 1)], last, tail_sem.at[0]
    )
    edge_load = pltpu.make_async_copy(fields.at[:, :, COLS - 1, main], edge, tail_sem.at[1])
    tail_load.start()

    def start_load(c, carry):
        load(c).start()
        return carry

    lax.fori_loop(0, CHANNELS, start_load, 0)
    edge_load.start()

    pl.semaphore_wait(barrier, len(greeted))
    def remote(source, target, index, peer):
        return pltpu.make_async_remote_copy(
            source, target, halo_send.at[index], halo_recv.at[index], device_id=peer, device_id_type=MESH
        )

    lat_up = {"lat": lax.max(lat - 1, 0)}
    lat_down = {"lat": lax.min(lat + 1, n_lat - 1)}
    east_copies = [
        remote(fields.at[:, :, 0, main], east, 0, west_id),
        remote(pack_col, got_col, 1, west_id),
    ]
    south_copies = [
        remote(fields.at[:, 0, :, main], south, 2, lat_up),
        remote(pack_row, got_row, 3, lat_up),
    ]
    west_copy = remote(fields.at[:, :, COLS - 1, main], west, 4, east_id)
    north_copy = remote(fields.at[:, ROWS - 1, :, main], north, 5, lat_down)

    @pl.when(lat > 0)
    def _():
        south_copies[0].start()

    east_copies[0].start()

    @pl.when(lat < n_lat - 1)
    def _():
        north_copy.start()

    west_copy.start()

    body[:, ROWS : ROWS + 1, 0:COLS, :] = jnp.zeros((CHANNELS, 1, COLS, LANES), F32)
    body[:, :, COLS : COLS + 8, :] = jnp.zeros((CHANNELS, ROWS + 1, 8, LANES), F32)
    acc_one[...] = jnp.zeros_like(acc_one)
    acc_two[...] = jnp.zeros_like(acc_two)

    tail_load.wait()
    wide_lane = iota((LANES, LANES), 1)
    merged = jnp.zeros((LANES, LANES), F32)
    for c in range(CHANNELS):
        for q in range(4):
            line = last[c, 4 * q : 4 * q + 4].reshape(LANES, 1)
            merged = jnp.where(wide_lane == 4 * c + q, jnp.broadcast_to(line, (LANES, LANES)), merged)
    tail_cells[...] = merged
    pack_row[...] = merged[0:COLS]
    sub8 = iota((8, LANES), 0)

    def column(ref_or_value, j):
        lines = [jnp.broadcast_to(ref_or_value[COLS * i + j : COLS * i + j + 1, :], (8, LANES)) for i in range(4)]
        result = lines[3]
        for i in range(3):
            result = jnp.where(sub8 == i, lines[i], result)
        return result

    pack_col[...] = column(tail_cells, 0)
    east_copies[1].start()

    @pl.when(lat > 0)
    def _():
        south_copies[1].start()

    count = 4 * CHANNELS
    tail = merged.T[:count]
    row, lane = iota((count, LANES), 0), iota((count, LANES), 1)
    right = tail * jnp.where(lane % COLS == COLS - 1, 0.0, pltpu.roll(tail, LANES - 1, 1))
    ahead = pltpu.roll(tail, LANES - COLS, 1)
    further = jnp.where(row % 4 == 3, 0.0, pltpu.roll(ahead, count - 1, 0))
    lower = tail * jnp.where(lane < LANES - COLS, ahead, further)
    for f, values in enumerate((tail, lower, right)):
        high = values.astype(BF16).astype(F32)
        low = values - high
        for pair in range(CHANNELS // 2):
            high8, low8 = high[8 * pair : 8 * pair + 8], low[8 * pair : 8 * pair + 8]
            first = jnp.where(sub8 < 4, high8, pltpu.roll(low8, 4, 0))
            second = jnp.where(sub8 < 4, pltpu.roll(high8, 4, 0), low8)
            for c, both in ((2 * pair, first), (2 * pair + 1, second)):
                for q in range(4):
                    part_q = jnp.where(sub8 % 4 == q, both, 0.0)
                    part_q = jnp.concatenate([part_q, jnp.zeros((8, LANES), F32)], axis=0)
                    tails_ref[f, c, :, LANES * q : LANES * q + LANES] = part_q.astype(BF16)
    own_one = sums(tail, tail)
    own_two = sums(lower, lower) + sums(right, right)

    zero = jnp.zeros((8, LANES), F32)

    def channel(c, carry):
        rest_one, rest_two = carry
        load(c).wait()
        value = body[c, 0:ROWS, 0:COLS, :]
        product, rest = self_product(flat(value), tails_ref[0, c])
        acc_one[...] += product
        rest_one += rest
        product, rest = self_product(flat(value * body[c, 1 : ROWS + 1, 0:COLS, :]), tails_ref[1, c])
        acc_two[...] += product
        rest_two += rest
        product, rest = self_product(flat(value * body[c, 0:ROWS, 1 : COLS + 1, :]), tails_ref[2, c])
        acc_two[...] += product
        rest_two += rest
        return rest_one, rest_two

    rest_one, rest_two = lax.fori_loop(0, CHANNELS, channel, (zero, zero), unroll=True)
    edge_load.wait()

    @pl.when(lat < n_lat - 1)
    def _():
        for copy in south_copies:
            copy.wait_recv()

    for copy in east_copies:
        copy.wait_recv()

    @pl.when(lat == n_lat - 1)
    def _():
        south[...] = jnp.zeros_like(south)
        got_row[...] = jnp.zeros_like(got_row)

    @pl.when(lat == 0)
    def _():
        north[...] = jnp.zeros_like(north)

    def spread(packed, lane):
        return jnp.broadcast_to(packed[:, lane : lane + 1], (8, LANES))

    row_pairs = pltpu.roll(tail_cells[LANES - COLS : LANES, :], LANES - 3, 1) * got_row[...]
    column_pairs = column(tail_cells, COLS - 1) * got_col[...]
    column_pairs = jnp.where(sub8 < 4, column_pairs, pltpu.roll(pltpu.roll(column_pairs, 4, 0), LANES - 1, 1))
    tails = [
        spread(row_pairs[8 * t : 8 * t + 8], 4 * c) for c in range(CHANNELS) for t in range(COLS // 8)
    ]
    tails += [spread(column_pairs, 4 * c + 2 * h) for c in range(CHANNELS) for h in range(2)]
    tails = jnp.concatenate(tails, axis=0)
    border = jnp.concatenate(
        [flat(body[:, ROWS - 1, 0:COLS, :] * south[...]), flat(edge[...] * east[...])], axis=0
    )
    product, rest = self_product(border)
    rest_two += rest
    cross_two = sums(border, tails)
    border_own = sums(tails, tails).sum(axis=0, keepdims=True)

    scale = 1.0 / cells_total
    total = (acc_one[...] + 2.0 * acc_two[...]) * scale
    rest = (rest_one + 2.0 * rest_two).sum(axis=0, keepdims=True) * scale
    square = total[:LANES] + product * (2.0 * scale)
    twisted = square[:, LANES:]
    full = square[:, :LANES] + (twisted + twisted.T)
    full += jnp.where(iota((LANES, LANES), 0) == iota((LANES, LANES), 1), rest, 0.0)
    cross = cross_two.sum(axis=0, keepdims=True) * (2.0 * scale)
    mixed = total[LANES : LANES + 8]
    mixed = mixed[:, :LANES] + jnp.where(sub8 < 4, mixed[:, LANES:], 0.0)
    cross += mixed.sum(axis=0, keepdims=True)
    own = (own_one + 2.0 * own_two).sum(axis=0, keepdims=True).sum(axis=1, keepdims=True)
    own = (jnp.broadcast_to(own, (1, LANES)) + 2.0 * border_own) * scale

    half = LANES // 2
    top, bottom = full[:half], full[half:]
    row, lane = iota((half, LANES), 0), iota((half, LANES), 1)
    folded = jnp.where((lane < half) & (row < lane), pltpu.roll(bottom, half, 1), top)
    diagonal = jnp.where(lane == row + half, bottom, 0.0).sum(axis=0, keepdims=True)
    extra = jnp.where(iota((1, LANES), 1) < half, own, diagonal)
    rows = half // n_lat
    for owner in range(n_lat):
        part[owner, 0:rows, :] = folded[owner * rows : (owner + 1) * rows]
        tail = cross if owner == 0 else extra if owner == 1 else jnp.zeros((1, LANES), F32)
        part[owner, rows : rows + 1, :] = tail

    def exchange(count, me, peer_of, device_of, source_of, buf, send, recv):
        def start(step, carry):
            peer = peer_of(step)
            pltpu.make_async_remote_copy(
                source_of(peer), buf.at[me], send.at[0], recv.at[0], device_id=device_of(peer), device_id_type=MESH
            ).start()
            return carry

        lax.fori_loop(1, count, start, 0)
        others = buf.at[pl.ds(0, count - 1)]
        pltpu.make_async_copy(others, others, recv.at[0]).wait()
        return pltpu.make_async_copy(others, others, send.at[0])

    def added(buf, count):
        result = buf[0]
        for index in range(1, count):
            result = result + buf[index]
        return result

    lat_buf[lat] = part[lat]
    pending = [exchange(
        n_lat, lat, lat_peer, lambda p: {"lat": p}, lambda p: part.at[p], lat_buf, lat_send, lat_recv
    )]
    y_buf[y] = added(lat_buf, n_lat)
    pending += [exchange(
        n_y, y, y_peer, lambda p: {"lon": p * n_z + z}, lambda p: y_buf.at[y], y_buf, y_send, y_recv
    )]
    z_buf[z] = added(y_buf, n_y)
    pending += [exchange(
        n_z, z, z_peer, lambda p: {"lon": y * n_z + p}, lambda p: z_buf.at[z], z_buf, z_send, z_recv
    )]
    all_buf[lat] = added(z_buf, n_z)
    pending += [exchange(
        n_lat, lat, lat_peer, lambda p: {"lat": p}, lambda p: all_buf.at[lat], all_buf, all_send, all_recv
    )]
    gram_out[...] = all_buf[...]

    @pl.when(lat > 0)
    def _():
        north_copy.wait_recv()
        for copy in south_copies:
            copy.wait_send()

    @pl.when(lat < n_lat - 1)
    def _():
        north_copy.wait_send()

    west_copy.wait_recv()
    for copy in [west_copy] + east_copies:
        copy.wait_send()
    for copy in pending:
        copy.wait()
    north_out[...] = north[...]
    south_out[...] = south[...]
    west_out[...] = west[...]
    east_out[...] = east[...]


def gram_call(fields, n_lat, n_lon):
    n_z = 8 if n_lon % 32 == 0 else max(n_lon // 2, 1)
    n_y = n_lon // n_z
    rows = LANES // 2 // n_lat + 1
    cells_total = 5 * CHANNELS * ROWS * n_lat * COLS * n_lon
    row_shape, col_shape = (CHANNELS, COLS, LANES), (CHANNELS, ROWS, LANES)
    chunk = (rows, LANES)
    dma = pltpu.SemaphoreType.DMA
    shapes = [(n_lat,) + chunk, row_shape, row_shape, col_shape, col_shape]
    vmem = pl.BlockSpec(memory_space=pltpu.VMEM)
    return pl.pallas_call(
        functools.partial(gram_kernel, (n_lat, n_y, n_z), cells_total),
        out_shape=[jax.ShapeDtypeStruct(shape, F32) for shape in shapes],
        in_specs=[pl.BlockSpec(memory_space=pltpu.HBM)],
        out_specs=[vmem] * 5,
        scratch_shapes=[
            pltpu.VMEM((CHANNELS, ROWS + 1, COLS + 8, LANES), F32),
            pltpu.VMEM((CHANNELS, ROWS, COLS, 1), F32),
            pltpu.VMEM(col_shape, F32),
            pltpu.VMEM(row_shape, F32),
            pltpu.VMEM(row_shape, F32),
            pltpu.VMEM(col_shape, F32),
            pltpu.VMEM(col_shape, F32),
        ]
        + [pltpu.VMEM((COLS, LANES), F32), pltpu.VMEM((8, LANES), F32)] * 2
        + [pltpu.VMEM((LANES, LANES), F32), pltpu.VMEM((3, CHANNELS, 16, 4 * LANES), BF16)]
        + [pltpu.VMEM((LANES + 16, 2 * LANES), F32)] * 2
        + [
            pltpu.VMEM((n_lat,) + chunk, F32),
            pltpu.VMEM((n_lat,) + chunk, F32),
            pltpu.VMEM((n_y,) + chunk, F32),
            pltpu.VMEM((n_z,) + chunk, F32),
            pltpu.VMEM((n_lat,) + chunk, F32),
            dma((CHANNELS,)), dma((2,)),
            dma((6,)), dma((6,)),
            dma((1,)), dma((1,)),
            dma((1,)), dma((1,)),
            dma((1,)), dma((1,)),
            dma((1,)), dma((1,)),
        ],
        compiler_params=pltpu.CompilerParams(
            collective_id=0, has_side_effects=True, vmem_limit_bytes=48 << 20
        ),
    )(fields)


def unfolded(gram):
    n_lat, rows, _ = gram.shape
    half = LANES // 2
    folded = jnp.concatenate([gram[owner, : rows - 1, :] for owner in range(n_lat)], axis=0)
    cross, extra = gram[0, rows - 1 : rows, :], gram[1, rows - 1 : rows, :]
    row, lane = iota((half, LANES), 0), iota((half, LANES), 1)
    top = jnp.where((lane < half) & (row <= lane), 0.0, folded)
    bottom = jnp.where((lane >= half) & (row < lane - half), pltpu.roll(folded, half, 1), 0.0)
    once = jnp.concatenate([top, bottom], axis=0)
    diagonal = jnp.concatenate(
        [jnp.where(lane == row, folded, 0.0), jnp.where(lane == row + half, jnp.broadcast_to(extra, (half, LANES)), 0.0)],
        axis=0,
    )
    full = once + once.T + diagonal
    row, lane = iota((LANES, LANES), 0), iota((LANES, LANES), 1)

    def column(line):
        return jnp.where(row == lane, jnp.broadcast_to(line, (LANES, LANES)), 0.0).sum(axis=1, keepdims=True)

    corner = extra[:, 0:1]
    shifted = pltpu.roll(pltpu.roll(full, LANES - 1, 0), LANES - 1, 1)
    line = jnp.where(iota((1, LANES), 1) == LANES - 1, corner, pltpu.roll(cross, LANES - 1, 1))
    shifted = jnp.where(lane == LANES - 1, column(line), shifted)
    shifted = jnp.where(row == LANES - 1, jnp.broadcast_to(line, (LANES, LANES)), shifted)
    identity = jnp.where(row == lane, 1.0, 0.0)
    first = jnp.where(lane == LANES - 1, column(cross), identity)
    low = jnp.where(row == LANES - 1, cross[:, 0:1], pltpu.roll(full, LANES - 1, 0)[:, 0:1])
    second = jnp.where(lane == LANES - 1, low, identity)
    return (full, first), (shifted, second)


def split_three(value):
    one = value.astype(BF16).astype(F32)
    two = (value - one).astype(BF16).astype(F32)
    return one, two, value - one - two


def eliminate(b, works, splats, first_row):
    start = b * 8
    sub, lane = iota((8, LANES), 0), iota((8, LANES), 1)
    upper = sub < 4
    for work, columns in zip(works, splats):
        block = pltpu.roll(work[b, :, 0:LANES], (LANES - start) % LANES, 1)
        for j in range(8):
            columns[j] = jnp.broadcast_to(block[:, j : j + 1], (8, LANES))

    def paired(first, second):
        return jnp.where(upper, jnp.broadcast_to(first, (8, LANES)), jnp.broadcast_to(second, (8, LANES)))

    entry = {}
    for i in range(8):
        for j in range(i, 8):
            entry[i, j] = paired(*[columns[j, i : i + 1, :] for columns in splats])
    left_rows = [paired(*[work[b, i : i + 1, 0:LANES] for work in works]) for i in range(8)]
    right_rows = [paired(*[work[b, i : i + 1, LANES : 2 * LANES] for work in works]) for i in range(8)]
    inverse = []
    for k in range(8):
        inverse.append(1.0 / entry[k, k])
        for i in range(k + 1, 8):
            factor = entry[k, i] * inverse[k]
            for j in range(i, 8):
                entry[i, j] = entry[i, j] - factor * entry[k, j]
            left_rows[i] = left_rows[i] - factor * left_rows[k]
            right_rows[i] = right_rows[i] - factor * right_rows[k]

    def gathered(rows):
        low, high = rows[0], rows[4]
        for k in range(1, 4):
            low = jnp.where(sub % 4 == k, rows[k], low)
            high = jnp.where(sub % 4 == k, rows[4 + k], high)
        return jnp.where(upper, low, pltpu.roll(high, 4, 0)), jnp.where(upper, pltpu.roll(low, 4, 0), high)

    below = slice(first_row // 8, LANES // 8)
    for work, pivots, done_left, done_right in zip(
        works, gathered(inverse), gathered(left_rows), gathered(right_rows)
    ):
        f1, f2, f3 = split_three(jnp.where(lane >= start + 8, done_left * pivots, 0.0))
        d1, d2, d3 = split_three(jnp.concatenate([done_left, done_right], axis=1))
        factors = jnp.concatenate([f1, f1, f2, f1, f2, f3], axis=0).T.astype(BF16)
        done = jnp.concatenate([d1, d2, d1, d3, d2, d1], axis=0).astype(BF16)
        update = jnp.dot(factors[first_row:], done, preferred_element_type=F32)
        root = jnp.sqrt(pivots)
        work[b, :, 0:LANES] = done_left * root
        work[b, :, LANES : 2 * LANES] = done_right * root
        work[below] = work[below] - update.reshape(-1, 8, 2 * LANES)


def accurate(left, right):
    return lax.dot_general(
        left, right, (((1,), (1,)), ((), ())), precision=lax.Precision.HIGHEST, preferred_element_type=F32
    )


def modes_kernel(
    fields, gram, north, south, west, east, modes, forward, backward,
    body, work_one, work_two, splat_one, splat_two, weights, first_column, plain, lower, left, right,
    load_sem, store_sem,
):
    works, splats = (work_one, work_two), (splat_one, splat_two)
    main = pl.ds(0, LANES)
    inner = pl.ds(1, ROWS)
    loads = [
        pltpu.make_async_copy(fields.at[:, :, :, main], body.at[:, inner, pl.ds(0, COLS), :], load_sem.at[0]),
        pltpu.make_async_copy(north, body.at[:, 0, pl.ds(0, COLS), :], load_sem.at[1]),
        pltpu.make_async_copy(south, body.at[:, ROWS + 1, pl.ds(0, COLS), :], load_sem.at[2]),
        pltpu.make_async_copy(fields.at[:, :, 0, main], first_column, load_sem.at[3]),
        pltpu.make_async_copy(east, body.at[:, inner, COLS, :], load_sem.at[4]),
    ]
    for copy in loads:
        copy.start()

    for work, (matrix, extended) in zip(works, unfolded(gram[...])):
        work[:, :, 0:LANES] = matrix.reshape(-1, 8, LANES)
        work[:, :, LANES : 2 * LANES] = extended.reshape(-1, 8, LANES)

    for phase in range(4):

        def step(b, carry):
            eliminate(b, works, splats, phase * 32)
            return carry

        lax.fori_loop(phase * 4, phase * 4 + 4, step, 0)

    row, lane = iota((LANES, LANES), 0), iota((LANES, LANES), 1)

    def parts(c):
        factor, extended = flat(works[c][:, :, 0:LANES]), flat(works[c][:, :, LANES : 2 * LANES])
        corner = jnp.where((row == LANES - 1) & (lane == LANES - 1), 1.0 / factor, 0.0)
        return factor, extended, jnp.where(lane == LANES - 1, corner, extended)

    factor, extended, inverse = parts(0)
    mixing = inverse.T
    high = mixing.astype(BF16)
    low = (mixing - high.astype(F32)).astype(BF16)
    line = jnp.concatenate([high, low], axis=1)
    weights[...] = jnp.concatenate([line, line], axis=0)

    for copy in loads:
        copy.wait()

    def mixed(value):
        both = jnp.dot(split_pair(value), weights[...], preferred_element_type=F32)
        return both[:, :LANES] + both[:, LANES:]

    inner_cols, outer_cols = pl.ds(0, COLS - 1), pl.ds(1, COLS - 1)

    def stores(c):
        return [
            pltpu.make_async_copy(plain.at[c], modes.at[c], store_sem.at[0, c]),
            pltpu.make_async_copy(lower.at[c, pl.ds(0, ROWS)], modes.at[CHANNELS + c], store_sem.at[1, c]),
            pltpu.make_async_copy(lower.at[c, pl.ds(1, ROWS)], modes.at[2 * CHANNELS + c], store_sem.at[2, c]),
            pltpu.make_async_copy(
                right.at[c, :, inner_cols, :], modes.at[3 * CHANNELS + c, :, outer_cols, :], store_sem.at[3, c]
            ),
            pltpu.make_async_copy(right.at[c], modes.at[4 * CHANNELS + c], store_sem.at[4, c]),
        ]

    first_store = pltpu.make_async_copy(
        left, modes.at[pl.ds(3 * CHANNELS, CHANNELS), :, 0, :], load_sem.at[0]
    )
    left[...] = mixed(flat(first_column[...] * west[...])).reshape((CHANNELS, ROWS, LANES))
    first_store.start()

    def channel(c, carry):
        value = body[c, 1 : ROWS + 1, 0:COLS, :]
        pairs = body[c, 0 : ROWS + 1, 0:COLS, :] * body[c, 1 : ROWS + 2, 0:COLS, :]
        beside = value * body[c, 1 : ROWS + 1, 1 : COLS + 1, :]
        both = mixed(jnp.concatenate([flat(value), flat(pairs), flat(beside)], axis=0))
        cells = ROWS * COLS
        plain[c] = both[:cells].reshape((ROWS, COLS, LANES))
        lower[c] = both[cells : 2 * cells + COLS].reshape((ROWS + 1, COLS, LANES))
        right[c] = both[2 * cells + COLS :].reshape((ROWS, COLS, LANES))
        for copy in stores(c):
            copy.start()
        return carry

    lax.fori_loop(0, CHANNELS, channel, 0, unroll=True)

    shifted = jnp.where(lane == LANES - 1, extended, pltpu.roll(factor, LANES - 1, 1))
    forward[...] = accurate(shifted, inverse)
    factor, extended, inverse = parts(1)
    mixed_block = jnp.where(lane == 0, pltpu.roll(extended, 1, 1), pltpu.roll(factor, 1, 1))
    backward[...] = accurate(mixed_block, inverse)

    def finish(c, carry):
        for copy in stores(c):
            copy.wait()
        return carry

    lax.fori_loop(0, CHANNELS, finish, 0)
    first_store.wait()


def modes_call(fields, gram, north, south, west, east):
    shape = (CHANNELS, ROWS, COLS, LANES)
    any_space = pl.BlockSpec(memory_space=pl.ANY)
    vmem = pl.BlockSpec(memory_space=pltpu.VMEM)
    return pl.pallas_call(
        modes_kernel,
        out_shape=[
            jax.ShapeDtypeStruct((5 * CHANNELS, ROWS, COLS, LANES), F32),
            jax.ShapeDtypeStruct((LANES, LANES), F32),
            jax.ShapeDtypeStruct((LANES, LANES), F32),
        ],
        in_specs=[pl.BlockSpec(memory_space=pltpu.HBM), vmem, any_space, any_space, vmem, any_space],
        out_specs=[any_space, vmem, vmem],
        scratch_shapes=[
            pltpu.VMEM((CHANNELS, ROWS + 2, COLS + 8, LANES), F32),
            pltpu.VMEM((LANES // 8, 8, 2 * LANES), F32),
            pltpu.VMEM((LANES // 8, 8, 2 * LANES), F32),
            pltpu.VMEM((8, 8, LANES), F32),
            pltpu.VMEM((8, 8, LANES), F32),
            pltpu.VMEM((2 * LANES, 2 * LANES), BF16),
            pltpu.VMEM((CHANNELS, ROWS, LANES), F32),
            pltpu.VMEM(shape, F32),
            pltpu.VMEM((CHANNELS, ROWS + 1, COLS, LANES), F32),
            pltpu.VMEM((CHANNELS, ROWS, LANES), F32),
            pltpu.VMEM(shape, F32),
            pltpu.SemaphoreType.DMA((5,)),
            pltpu.SemaphoreType.DMA((5, CHANNELS)),
        ],
        compiler_params=pltpu.CompilerParams(vmem_limit_bytes=48 << 20),
    )(fields, gram, north, south, west, east)


def shards(fields):
    cells = pltpu.with_memory_space_constraint(fields.transpose(1, 2, 3, 0), pltpu.HBM)
    gram, north, south, west, east = gram_call(cells, lax.axis_size("lat"), lax.axis_size("lon"))
    return tuple(modes_call(cells, gram, north, south, west, east))


def solution(mesh):
    return jax.shard_map(
        shards,
        mesh=mesh,
        in_specs=(P(None, None, "lat", "lon"),),
        out_specs=(P(None, "lat", "lon", None), P(), P()),
        check_vma=False,
    )
```

```python
import functools

import jax
import jax.numpy as jnp
from jax import lax
from jax.experimental import pallas as pl
from jax.experimental.pallas import tpu as pltpu
from jax.sharding import PartitionSpec as P

F32, BF16 = jnp.float32, jnp.bfloat16
MESH = pl.DeviceIdType.MESH
CHANNELS, ROWS, COLS, LANES = 6, 16, 32, 128


def split_pair(value):
    high = value.astype(BF16)
    low = (value - high.astype(F32)).astype(BF16)
    return jnp.concatenate([high, low], axis=-1)


def flat(value):
    return value.reshape(-1, value.shape[-1])


def iota(shape, dim):
    return lax.broadcasted_iota(jnp.int32, shape, dim)


def sums(value, other):
    return (value * other).reshape(-1, 8, LANES).sum(axis=0)


def self_product(value, tails=None):
    high = value.astype(BF16)
    rest = value - high.astype(F32)
    pair = jnp.concatenate([high, rest.astype(BF16)], axis=-1)
    turned = high.T
    squares = pair[:, LANES:] * pair[:, LANES:]
    squares = squares.reshape(-1, 16, LANES)
    count = squares.shape[0]
    total = jnp.zeros((8, LANES), F32)
    for first in range(0, count, 8):
        group = [squares[index] for index in range(first, min(first + 8, count))]
        while len(group) > 1:
            group = [left + right for left, right in zip(group[::2], group[1::2])] + group[len(group) // 2 * 2 :]
        total += group[0].astype(F32).reshape(2, 8, LANES).sum(axis=0)
    if tails is not None:
        turned = jnp.concatenate([turned, tails], axis=0)
    return jnp.dot(turned, pair, preferred_element_type=F32), total


def gram_kernel(
    sizes, cells_total, fields,
    gram_out, north_out, south_out, west_out, east_out,
    body, last, edge, north, south, west, east,
    pack_row, pack_col, got_row, got_col, tail_cells, tails_ref,
    acc_one, acc_two, part, lat_buf, y_buf, z_buf, all_buf,
    load_sem, tail_sem, halo_send, halo_recv, lat_send, lat_recv, y_send, y_recv, z_send, z_recv, all_send, all_recv,
):
    n_lat, n_y, n_z = sizes
    n_lon = n_y * n_z
    lat, lon = lax.axis_index("lat"), lax.axis_index("lon")
    y, z = lon // n_z, lon % n_z
    above, below = lon - 1 + n_lon, lon + 1
    west_id, east_id = {"lon": above % n_lon}, {"lon": below % n_lon}

    def lat_peer(step):
        return (lat + step) % n_lat

    def y_peer(step):
        return (y + step) % n_y

    def z_peer(step):
        return (z + step) % n_z

    main = pl.ds(0, LANES)

    def load(c):
        return pltpu.make_async_copy(
            fields.at[c, :, :, main], body.at[c, pl.ds(0, ROWS), pl.ds(0, COLS), :], load_sem.at[c]
        )

    tail_load = pltpu.make_async_copy(
        fields.at[:, :, :, pl.ds(LANES, 1)], last, tail_sem.at[0]
    )
    edge_load = pltpu.make_async_copy(fields.at[:, :, COLS - 1, main], edge, tail_sem.at[1])
    tail_load.start()

    def start_load(c, carry):
        load(c).start()
        return carry

    lax.fori_loop(0, CHANNELS, start_load, 0)
    edge_load.start()

    barrier = pltpu.get_barrier_semaphore()
    greeted = [west_id, east_id]
    greeted += [{"lat": lat_peer(step)} for step in range(1, n_lat)]
    greeted += [{"lon": y_peer(step) * n_z + z} for step in range(1, n_y)]
    greeted += [{"lon": y * n_z + z_peer(step)} for step in range(1, n_z)]
    for peer in greeted:
        pl.semaphore_signal(barrier, inc=1, device_id=peer, device_id_type=MESH)

    pl.semaphore_wait(barrier, len(greeted))
    def remote(source, target, index, peer):
        return pltpu.make_async_remote_copy(
            source, target, halo_send.at[index], halo_recv.at[index], device_id=peer, device_id_type=MESH
        )

    lat_up = {"lat": lax.max(lat - 1, 0)}
    lat_down = {"lat": lax.min(lat + 1, n_lat - 1)}
    east_copies = [
        remote(fields.at[:, :, 0, main], east, 0, west_id),
        remote(pack_col, got_col, 1, west_id),
    ]
    south_copies = [
        remote(fields.at[:, 0, :, main], south, 2, lat_up),
        remote(pack_row, got_row, 3, lat_up),
    ]
    west_copy = remote(fields.at[:, :, COLS - 1, main], west, 4, east_id)
    north_copy = remote(fields.at[:, ROWS - 1, :, main], north, 5, lat_down)

    @pl.when(lat > 0)
    def _():
        south_copies[0].start()

    east_copies[0].start()

    @pl.when(lat < n_lat - 1)
    def _():
        north_copy.start()

    west_copy.start()

    body[:, ROWS : ROWS + 1, 0:COLS, :] = jnp.zeros((CHANNELS, 1, COLS, LANES), F32)
    body[:, :, COLS : COLS + 8, :] = jnp.zeros((CHANNELS, ROWS + 1, 8, LANES), F32)
    acc_one[...] = jnp.zeros_like(acc_one)
    acc_two[...] = jnp.zeros_like(acc_two)

    tail_load.wait()
    wide_lane = iota((LANES, LANES), 1)
    merged = jnp.zeros((LANES, LANES), F32)
    for c in range(CHANNELS):
        for q in range(4):
            line = last[c, 4 * q : 4 * q + 4].reshape(LANES, 1)
            merged = jnp.where(wide_lane == 4 * c + q, jnp.broadcast_to(line, (LANES, LANES)), merged)
    tail_cells[...] = merged
    pack_row[...] = merged[0:COLS]
    sub8 = iota((8, LANES), 0)

    def column(ref_or_value, j):
        lines = [jnp.broadcast_to(ref_or_value[COLS * i + j : COLS * i + j + 1, :], (8, LANES)) for i in range(4)]
        result = lines[3]
        for i in range(3):
            result = jnp.where(sub8 == i, lines[i], result)
        return result

    pack_col[...] = column(tail_cells, 0)
    east_copies[1].start()

    @pl.when(lat > 0)
    def _():
        south_copies[1].start()

    count = 4 * CHANNELS
    tail = merged.T[:count]
    row, lane = iota((count, LANES), 0), iota((count, LANES), 1)
    right = tail * jnp.where(lane % COLS == COLS - 1, 0.0, pltpu.roll(tail, LANES - 1, 1))
    ahead = pltpu.roll(tail, LANES - COLS, 1)
    further = jnp.where(row % 4 == 3, 0.0, pltpu.roll(ahead, count - 1, 0))
    lower = tail * jnp.where(lane < LANES - COLS, ahead, further)
    for f, values in enumerate((tail, lower, right)):
        high = values.astype(BF16).astype(F32)
        low = values - high
        for pair in range(CHANNELS // 2):
            high8, low8 = high[8 * pair : 8 * pair + 8], low[8 * pair : 8 * pair + 8]
            first = jnp.where(sub8 < 4, high8, pltpu.roll(low8, 4, 0))
            second = jnp.where(sub8 < 4, pltpu.roll(high8, 4, 0), low8)
            for c, both in ((2 * pair, first), (2 * pair + 1, second)):
                for q in range(4):
                    part_q = jnp.where(sub8 % 4 == q, both, 0.0)
                    part_q = jnp.concatenate([part_q, jnp.zeros((8, LANES), F32)], axis=0)
                    tails_ref[f, c, :, LANES * q : LANES * q + LANES] = part_q.astype(BF16)
    own_one = sums(tail, tail)
    own_two = sums(lower, lower) + sums(right, right)

    zero = jnp.zeros((8, LANES), F32)

    def channel(c, carry):
        rest_one, rest_two = carry
        load(c).wait()
        value = body[c, 0:ROWS, 0:COLS, :]
        product, rest = self_product(flat(value), tails_ref[0, c])
        acc_one[...] += product
        rest_one += rest
        product, rest = self_product(flat(value * body[c, 1 : ROWS + 1, 0:COLS, :]), tails_ref[1, c])
        acc_two[...] += product
        rest_two += rest
        product, rest = self_product(flat(value * body[c, 0:ROWS, 1 : COLS + 1, :]), tails_ref[2, c])
        acc_two[...] += product
        rest_two += rest
        return rest_one, rest_two

    rest_one, rest_two = lax.fori_loop(0, CHANNELS, channel, (zero, zero), unroll=True)
    edge_load.wait()

    @pl.when(lat < n_lat - 1)
    def _():
        for copy in south_copies:
            copy.wait_recv()

    for copy in east_copies:
        copy.wait_recv()

    @pl.when(lat == n_lat - 1)
    def _():
        south[...] = jnp.zeros_like(south)
        got_row[...] = jnp.zeros_like(got_row)

    @pl.when(lat == 0)
    def _():
        north[...] = jnp.zeros_like(north)

    def spread(packed, lane):
        return jnp.broadcast_to(packed[:, lane : lane + 1], (8, LANES))

    row_pairs = pltpu.roll(tail_cells[LANES - COLS : LANES, :], LANES - 3, 1) * got_row[...]
    column_pairs = column(tail_cells, COLS - 1) * got_col[...]
    column_pairs = jnp.where(sub8 < 4, column_pairs, pltpu.roll(pltpu.roll(column_pairs, 4, 0), LANES - 1, 1))
    tails = [
        spread(row_pairs[8 * t : 8 * t + 8], 4 * c) for c in range(CHANNELS) for t in range(COLS // 8)
    ]
    tails += [spread(column_pairs, 4 * c + 2 * h) for c in range(CHANNELS) for h in range(2)]
    tails = jnp.concatenate(tails, axis=0)
    border = jnp.concatenate(
        [flat(body[:, ROWS - 1, 0:COLS, :] * south[...]), flat(edge[...] * east[...])], axis=0
    )
    product, rest = self_product(border)
    rest_two += rest
    cross_two = sums(border, tails)
    border_own = sums(tails, tails).sum(axis=0, keepdims=True)

    scale = 1.0 / cells_total
    total = (acc_one[...] + 2.0 * acc_two[...]) * scale
    rest = (rest_one + 2.0 * rest_two).sum(axis=0, keepdims=True) * scale
    square = total[:LANES] + product * (2.0 * scale)
    twisted = square[:, LANES:]
    full = square[:, :LANES] + (twisted + twisted.T)
    full += jnp.where(iota((LANES, LANES), 0) == iota((LANES, LANES), 1), rest, 0.0)
    cross = cross_two.sum(axis=0, keepdims=True) * (2.0 * scale)
    mixed = total[LANES : LANES + 8]
    mixed = mixed[:, :LANES] + jnp.where(sub8 < 4, mixed[:, LANES:], 0.0)
    cross += mixed.sum(axis=0, keepdims=True)
    own = (own_one + 2.0 * own_two).sum(axis=0, keepdims=True).sum(axis=1, keepdims=True)
    own = (jnp.broadcast_to(own, (1, LANES)) + 2.0 * border_own) * scale

    half = LANES // 2
    top, bottom = full[:half], full[half:]
    row, lane = iota((half, LANES), 0), iota((half, LANES), 1)
    folded = jnp.where((lane < half) & (row < lane), pltpu.roll(bottom, half, 1), top)
    diagonal = jnp.where(lane == row + half, bottom, 0.0).sum(axis=0, keepdims=True)
    extra = jnp.where(iota((1, LANES), 1) < half, own, diagonal)
    rows = half // n_lat
    for owner in range(n_lat):
        part[owner, 0:rows, :] = folded[owner * rows : (owner + 1) * rows]
        tail = cross if owner == 0 else extra if owner == 1 else jnp.zeros((1, LANES), F32)
        part[owner, rows : rows + 1, :] = tail

    def exchange(count, me, peer_of, device_of, source_of, buf, send, recv):
        def start(step):
            peer = peer_of(step)
            pltpu.make_async_remote_copy(
                source_of(peer), buf.at[me], send.at[0], recv.at[0], device_id=device_of(peer), device_id_type=MESH
            ).start()

        start(count // 2)

        def start_two(t, carry):
            start(count // 2 + t)
            start(count // 2 - t)
            return carry

        lax.fori_loop(1, count // 2, start_two, 0)
        others = buf.at[pl.ds(0, count - 1)]
        pltpu.make_async_copy(others, others, recv.at[0]).wait()
        return pltpu.make_async_copy(others, others, send.at[0])

    def added(buf, count):
        result = buf[0]
        for index in range(1, count):
            result = result + buf[index]
        return result

    lat_buf[lat] = part[lat]
    pending = [exchange(
        n_lat, lat, lat_peer, lambda p: {"lat": p}, lambda p: part.at[p], lat_buf, lat_send, lat_recv
    )]
    y_buf[y] = added(lat_buf, n_lat)
    pending += [exchange(
        n_y, y, y_peer, lambda p: {"lon": p * n_z + z}, lambda p: y_buf.at[y], y_buf, y_send, y_recv
    )]
    z_buf[z] = added(y_buf, n_y)
    pending += [exchange(
        n_z, z, z_peer, lambda p: {"lon": y * n_z + p}, lambda p: z_buf.at[z], z_buf, z_send, z_recv
    )]
    all_buf[lat] = added(z_buf, n_z)
    pending += [exchange(
        n_lat, lat, lat_peer, lambda p: {"lat": p}, lambda p: all_buf.at[lat], all_buf, all_send, all_recv
    )]
    gram_out[...] = all_buf[...]

    @pl.when(lat > 0)
    def _():
        north_copy.wait_recv()
        for copy in south_copies:
            copy.wait_send()

    @pl.when(lat < n_lat - 1)
    def _():
        north_copy.wait_send()

    west_copy.wait_recv()
    for copy in [west_copy] + east_copies:
        copy.wait_send()
    for copy in pending:
        copy.wait()
    north_out[...] = north[...]
    south_out[...] = south[...]
    west_out[...] = west[...]
    east_out[...] = east[...]


def gram_call(fields, n_lat, n_lon):
    n_z = 8 if n_lon % 32 == 0 else max(n_lon // 2, 1)
    n_y = n_lon // n_z
    rows = LANES // 2 // n_lat + 1
    cells_total = 5 * CHANNELS * ROWS * n_lat * COLS * n_lon
    row_shape, col_shape = (CHANNELS, COLS, LANES), (CHANNELS, ROWS, LANES)
    chunk = (rows, LANES)
    dma = pltpu.SemaphoreType.DMA
    shapes = [(n_lat,) + chunk, row_shape, row_shape, col_shape, col_shape]
    vmem = pl.BlockSpec(memory_space=pltpu.VMEM)
    return pl.pallas_call(
        functools.partial(gram_kernel, (n_lat, n_y, n_z), cells_total),
        out_shape=[jax.ShapeDtypeStruct(shape, F32) for shape in shapes],
        in_specs=[pl.BlockSpec(memory_space=pltpu.HBM)],
        out_specs=[vmem] * 5,
        scratch_shapes=[
            pltpu.VMEM((CHANNELS, ROWS + 1, COLS + 8, LANES), F32),
            pltpu.VMEM((CHANNELS, ROWS, COLS, 1), F32),
            pltpu.VMEM(col_shape, F32),
            pltpu.VMEM(row_shape, F32),
            pltpu.VMEM(row_shape, F32),
            pltpu.VMEM(col_shape, F32),
            pltpu.VMEM(col_shape, F32),
        ]
        + [pltpu.VMEM((COLS, LANES), F32), pltpu.VMEM((8, LANES), F32)] * 2
        + [pltpu.VMEM((LANES, LANES), F32), pltpu.VMEM((3, CHANNELS, 16, 4 * LANES), BF16)]
        + [pltpu.VMEM((LANES + 16, 2 * LANES), F32)] * 2
        + [
            pltpu.VMEM((n_lat,) + chunk, F32),
            pltpu.VMEM((n_lat,) + chunk, F32),
            pltpu.VMEM((n_y,) + chunk, F32),
            pltpu.VMEM((n_z,) + chunk, F32),
            pltpu.VMEM((n_lat,) + chunk, F32),
            dma((CHANNELS,)), dma((2,)),
            dma((6,)), dma((6,)),
            dma((1,)), dma((1,)),
            dma((1,)), dma((1,)),
            dma((1,)), dma((1,)),
            dma((1,)), dma((1,)),
        ],
        compiler_params=pltpu.CompilerParams(
            collective_id=0, has_side_effects=True, vmem_limit_bytes=48 << 20
        ),
    )(fields)


def unfolded(gram):
    n_lat, rows, _ = gram.shape
    half = LANES // 2
    folded = jnp.concatenate([gram[owner, : rows - 1, :] for owner in range(n_lat)], axis=0)
    cross, extra = gram[0, rows - 1 : rows, :], gram[1, rows - 1 : rows, :]
    row, lane = iota((half, LANES), 0), iota((half, LANES), 1)
    top = jnp.where((lane < half) & (row <= lane), 0.0, folded)
    bottom = jnp.where((lane >= half) & (row < lane - half), pltpu.roll(folded, half, 1), 0.0)
    once = jnp.concatenate([top, bottom], axis=0)
    diagonal = jnp.concatenate(
        [jnp.where(lane == row, folded, 0.0), jnp.where(lane == row + half, jnp.broadcast_to(extra, (half, LANES)), 0.0)],
        axis=0,
    )
    full = once + once.T + diagonal
    row, lane = iota((LANES, LANES), 0), iota((LANES, LANES), 1)

    def column(line):
        return jnp.where(row == lane, jnp.broadcast_to(line, (LANES, LANES)), 0.0).sum(axis=1, keepdims=True)

    corner = extra[:, 0:1]
    shifted = pltpu.roll(pltpu.roll(full, LANES - 1, 0), LANES - 1, 1)
    line = jnp.where(iota((1, LANES), 1) == LANES - 1, corner, pltpu.roll(cross, LANES - 1, 1))
    shifted = jnp.where(lane == LANES - 1, column(line), shifted)
    shifted = jnp.where(row == LANES - 1, jnp.broadcast_to(line, (LANES, LANES)), shifted)
    identity = jnp.where(row == lane, 1.0, 0.0)
    first = jnp.where(lane == LANES - 1, column(cross), identity)
    low = jnp.where(row == LANES - 1, cross[:, 0:1], pltpu.roll(full, LANES - 1, 0)[:, 0:1])
    second = jnp.where(lane == LANES - 1, low, identity)
    return (full, first), (shifted, second)


def split_three(value):
    one = value.astype(BF16).astype(F32)
    two = (value - one).astype(BF16).astype(F32)
    return one, two, value - one - two


def eliminate(b, works, splats, nears, turned_refs, done_refs, first_row):
    start = b * 8
    sub, lane = iota((8, LANES), 0), iota((8, LANES), 1)
    upper = sub < 4
    left_part, right_part = slice(0, LANES), slice(LANES, 2 * LANES)
    after = lax.min(b + 1, LANES // 8 - 1)

    def joined(first, second):
        return [jnp.where(upper, first, pltpu.roll(second, 4, 0)), jnp.where(upper, pltpu.roll(first, 4, 0), second)]

    following = []
    for work, turned, done in zip(works, turned_refs, done_refs):
        small = jnp.dot(turned[after].astype(BF16), done[...], preferred_element_type=F32)
        following.append(work[after] - small)
    below = slice(first_row // 8, LANES // 8)
    for work, turned, done in zip(works, turned_refs, done_refs):
        update = jnp.dot(flat(turned[below]).astype(BF16), done[...], preferred_element_type=F32)
        work[below] = work[below] - update.reshape(-1, 8, 2 * LANES)
    next_left = joined(*[rows[:, left_part] for rows in following])
    next_right = joined(*[rows[:, right_part] for rows in following])

    shift = (LANES - start) % LANES

    def columns_of(rows, first):
        block = pltpu.roll(rows, shift, 1)
        return {j: jnp.broadcast_to(block[:, j : j + 1], (8, LANES)) for j in range(first, 8)}

    for h in range(2):
        for j, column in columns_of(nears[h, :, left_part], 4 * h).items():
            splats[h, j] = column

    def paired(ref, row):
        first, second = ref[row : row + 1, :], ref[4 + row : 5 + row, :]
        return jnp.where(upper, jnp.broadcast_to(first, (8, LANES)), jnp.broadcast_to(second, (8, LANES)))

    entry = {}
    for i in range(8):
        for j in range(i, 8):
            entry[i, j] = paired(splats.at[i // 4, j], i % 4)
    left_rows = [paired(nears.at[i // 4, :, left_part], i % 4) for i in range(8)]
    right_rows = [paired(nears.at[i // 4, :, right_part], i % 4) for i in range(8)]
    next_columns = [columns_of(rows, 0) for rows in next_left]
    inverse = []
    for k in range(8):
        inverse.append(1.0 / entry[k, k])
        for i in range(k + 1, 8):
            factor = entry[k, i] * inverse[k]
            for j in range(i, 8):
                entry[i, j] = entry[i, j] - factor * entry[k, j]
            left_rows[i] = left_rows[i] - factor * left_rows[k]
            right_rows[i] = right_rows[i] - factor * right_rows[k]
        for h in range(2):
            factor = next_columns[h][k] * inverse[k]
            for j in range(k + 1, 8):
                next_columns[h][j] = next_columns[h][j] - factor * entry[k, j]
            next_left[h] = next_left[h] - factor * left_rows[k]
            next_right[h] = next_right[h] - factor * right_rows[k]
    for h in range(2):
        nears[h, :, left_part] = next_left[h]
        nears[h, :, right_part] = next_right[h]

    def gathered(rows):
        low, high = rows[0], rows[4]
        for k in range(1, 4):
            low = jnp.where(sub % 4 == k, rows[k], low)
            high = jnp.where(sub % 4 == k, rows[4 + k], high)
        return joined(low, high)

    for work, turned, done, pivots, done_left, done_right in zip(
        works, turned_refs, done_refs, gathered(inverse), gathered(left_rows), gathered(right_rows)
    ):
        f1, f2, f3 = split_three(jnp.where(lane >= start + 16, done_left * pivots, 0.0))
        d1, d2, d3 = split_three(jnp.concatenate([done_left, done_right], axis=1))
        turned[...] = jnp.concatenate([f1, f1, f2, f1, f2, f3], axis=0).T.reshape(-1, 8, 48)
        done[...] = jnp.concatenate([d1, d2, d1, d3, d2, d1], axis=0).astype(BF16)
        root = jnp.sqrt(pivots)
        work[b, :, left_part] = done_left * root
        work[b, :, right_part] = done_right * root


def accurate(left, right):
    return lax.dot_general(
        left, right, (((1,), (1,)), ((), ())), precision=lax.Precision.HIGHEST, preferred_element_type=F32
    )


def modes_kernel(
    fields, gram, north, south, west, east, modes, forward, backward,
    body, work_one, work_two, splat, near, turned_one, turned_two, done_one, done_two, weights, first_column, plain, lower, left, right,
    load_sem, store_sem,
):
    works, turned, done = (work_one, work_two), (turned_one, turned_two), (done_one, done_two)
    main = pl.ds(0, LANES)
    inner = pl.ds(1, ROWS)
    loads = [
        pltpu.make_async_copy(fields.at[:, :, :, main], body.at[:, inner, pl.ds(0, COLS), :], load_sem.at[0]),
        pltpu.make_async_copy(north, body.at[:, 0, pl.ds(0, COLS), :], load_sem.at[1]),
        pltpu.make_async_copy(south, body.at[:, ROWS + 1, pl.ds(0, COLS), :], load_sem.at[2]),
        pltpu.make_async_copy(fields.at[:, :, 0, main], first_column, load_sem.at[3]),
        pltpu.make_async_copy(east, body.at[:, inner, COLS, :], load_sem.at[4]),
    ]
    for copy in loads:
        copy.start()

    for work, (matrix, extended) in zip(works, unfolded(gram[...])):
        work[:, :, 0:LANES] = matrix.reshape(-1, 8, LANES)
        work[:, :, LANES : 2 * LANES] = extended.reshape(-1, 8, LANES)

    upper = iota((8, LANES), 0) < 4
    for part in range(0, 2 * LANES, LANES):
        first, second = [work[0, :, part : part + LANES] for work in works]
        near[0, :, part : part + LANES] = jnp.where(upper, first, pltpu.roll(second, 4, 0))
        near[1, :, part : part + LANES] = jnp.where(upper, pltpu.roll(first, 4, 0), second)
    for ref in turned + done:
        ref[...] = jnp.zeros_like(ref)

    for phase in range(4):

        def step(b, carry):
            eliminate(b, works, splat, near, turned, done, phase * 32)
            return carry

        lax.fori_loop(phase * 4, phase * 4 + 4, step, 0)

    row, lane = iota((LANES, LANES), 0), iota((LANES, LANES), 1)

    def parts(c):
        factor, extended = flat(works[c][:, :, 0:LANES]), flat(works[c][:, :, LANES : 2 * LANES])
        corner = jnp.where((row == LANES - 1) & (lane == LANES - 1), 1.0 / factor, 0.0)
        return factor, extended, jnp.where(lane == LANES - 1, corner, extended)

    factor, extended, inverse = parts(0)
    mixing = inverse.T
    high = mixing.astype(BF16)
    low = (mixing - high.astype(F32)).astype(BF16)
    line = jnp.concatenate([high, low], axis=1)
    weights[...] = jnp.concatenate([line, line], axis=0)

    for copy in loads:
        copy.wait()

    def mixed(value):
        both = jnp.dot(split_pair(value), weights[...], preferred_element_type=F32)
        return both[:, :LANES] + both[:, LANES:]

    inner_cols, outer_cols = pl.ds(0, COLS - 1), pl.ds(1, COLS - 1)

    def stores(c):
        return [
            pltpu.make_async_copy(plain.at[c], modes.at[c], store_sem.at[0, c]),
            pltpu.make_async_copy(lower.at[c, pl.ds(0, ROWS)], modes.at[CHANNELS + c], store_sem.at[1, c]),
            pltpu.make_async_copy(lower.at[c, pl.ds(1, ROWS)], modes.at[2 * CHANNELS + c], store_sem.at[2, c]),
            pltpu.make_async_copy(
                right.at[c, :, inner_cols, :], modes.at[3 * CHANNELS + c, :, outer_cols, :], store_sem.at[3, c]
            ),
            pltpu.make_async_copy(right.at[c], modes.at[4 * CHANNELS + c], store_sem.at[4, c]),
        ]

    first_store = pltpu.make_async_copy(
        left, modes.at[pl.ds(3 * CHANNELS, CHANNELS), :, 0, :], load_sem.at[0]
    )
    left[...] = mixed(flat(first_column[...] * west[...])).reshape((CHANNELS, ROWS, LANES))
    first_store.start()

    def channel(c, carry):
        value = body[c, 1 : ROWS + 1, 0:COLS, :]
        pairs = body[c, 0 : ROWS + 1, 0:COLS, :] * body[c, 1 : ROWS + 2, 0:COLS, :]
        beside = value * body[c, 1 : ROWS + 1, 1 : COLS + 1, :]
        both = mixed(jnp.concatenate([flat(value), flat(pairs), flat(beside)], axis=0))
        cells = ROWS * COLS
        plain[c] = both[:cells].reshape((ROWS, COLS, LANES))
        lower[c] = both[cells : 2 * cells + COLS].reshape((ROWS + 1, COLS, LANES))
        right[c] = both[2 * cells + COLS :].reshape((ROWS, COLS, LANES))
        for copy in stores(c):
            copy.start()
        return carry

    lax.fori_loop(0, CHANNELS, channel, 0, unroll=True)

    shifted = jnp.where(lane == LANES - 1, extended, pltpu.roll(factor, LANES - 1, 1))
    forward[...] = accurate(shifted, inverse)
    factor, extended, inverse = parts(1)
    mixed_block = jnp.where(lane == 0, pltpu.roll(extended, 1, 1), pltpu.roll(factor, 1, 1))
    backward[...] = accurate(mixed_block, inverse)

    def finish(c, carry):
        for copy in stores(c):
            copy.wait()
        return carry

    lax.fori_loop(0, CHANNELS, finish, 0)
    first_store.wait()


def modes_call(fields, gram, north, south, west, east):
    shape = (CHANNELS, ROWS, COLS, LANES)
    any_space = pl.BlockSpec(memory_space=pl.ANY)
    vmem = pl.BlockSpec(memory_space=pltpu.VMEM)
    return pl.pallas_call(
        modes_kernel,
        out_shape=[
            jax.ShapeDtypeStruct((5 * CHANNELS, ROWS, COLS, LANES), F32),
            jax.ShapeDtypeStruct((LANES, LANES), F32),
            jax.ShapeDtypeStruct((LANES, LANES), F32),
        ],
        in_specs=[pl.BlockSpec(memory_space=pltpu.HBM), vmem, any_space, any_space, vmem, any_space],
        out_specs=[any_space, vmem, vmem],
        scratch_shapes=[
            pltpu.VMEM((CHANNELS, ROWS + 2, COLS + 8, LANES), F32),
            pltpu.VMEM((LANES // 8, 8, 2 * LANES), F32),
            pltpu.VMEM((LANES // 8, 8, 2 * LANES), F32),
            pltpu.VMEM((2, 8, 8, LANES), F32),
            pltpu.VMEM((2, 8, 2 * LANES), F32),
            pltpu.VMEM((LANES // 8, 8, 48), F32),
            pltpu.VMEM((LANES // 8, 8, 48), F32),
            pltpu.VMEM((48, 2 * LANES), BF16),
            pltpu.VMEM((48, 2 * LANES), BF16),
            pltpu.VMEM((2 * LANES, 2 * LANES), BF16),
            pltpu.VMEM((CHANNELS, ROWS, LANES), F32),
            pltpu.VMEM(shape, F32),
            pltpu.VMEM((CHANNELS, ROWS + 1, COLS, LANES), F32),
            pltpu.VMEM((CHANNELS, ROWS, LANES), F32),
            pltpu.VMEM(shape, F32),
            pltpu.SemaphoreType.DMA((5,)),
            pltpu.SemaphoreType.DMA((5, CHANNELS)),
        ],
        compiler_params=pltpu.CompilerParams(vmem_limit_bytes=48 << 20),
    )(fields, gram, north, south, west, east)


def shards(fields):
    cells = pltpu.with_memory_space_constraint(fields.transpose(1, 2, 3, 0), pltpu.HBM)
    gram, north, south, west, east = gram_call(cells, lax.axis_size("lat"), lax.axis_size("lon"))
    return tuple(modes_call(cells, gram, north, south, west, east))


def solution(mesh):
    return jax.shard_map(
        shards,
        mesh=mesh,
        in_specs=(P(None, None, "lat", "lon"),),
        out_specs=(P(None, "lat", "lon", None), P(), P()),
        check_vma=False,
    )
```

```python
import functools

import jax
import jax.numpy as jnp
from jax import lax
from jax.experimental import pallas as pl
from jax.experimental.pallas import tpu as pltpu
from jax.sharding import PartitionSpec as P

F32, BF16 = jnp.float32, jnp.bfloat16
MESH = pl.DeviceIdType.MESH
CHANNELS, ROWS, COLS, LANES = 6, 16, 32, 128


def split_pair(value):
    high = value.astype(BF16)
    low = (value - high.astype(F32)).astype(BF16)
    return jnp.concatenate([high, low], axis=-1)


def flat(value):
    return value.reshape(-1, value.shape[-1])


def iota(shape, dim):
    return lax.broadcasted_iota(jnp.int32, shape, dim)


def sums(value, other):
    return (value * other).reshape(-1, 8, LANES).sum(axis=0)


def self_product(value, tails=None):
    high = value.astype(BF16)
    rest = value - high.astype(F32)
    pair = jnp.concatenate([high, rest.astype(BF16)], axis=-1)
    turned = high.T
    squares = pair[:, LANES:] * pair[:, LANES:]
    squares = squares.reshape(-1, 16, LANES)
    count = squares.shape[0]
    total = jnp.zeros((8, LANES), F32)
    for first in range(0, count, 8):
        group = [squares[index] for index in range(first, min(first + 8, count))]
        while len(group) > 1:
            group = [left + right for left, right in zip(group[::2], group[1::2])] + group[len(group) // 2 * 2 :]
        total += group[0].astype(F32).reshape(2, 8, LANES).sum(axis=0)
    if tails is not None:
        turned = jnp.concatenate([turned, tails], axis=0)
    return jnp.dot(turned, pair, preferred_element_type=F32), total


def gram_kernel(
    sizes, cells_total, fields,
    gram_out, north_out, south_out, west_out, east_out,
    body, last, edge, north, south, west, east,
    pack_row, pack_col, got_row, got_col, tail_cells, tails_ref,
    acc_one, acc_two, part, lat_buf, y_buf, z_buf, all_buf,
    relay_sem, load_sem, tail_sem, halo_send, halo_recv, lat_send, lat_recv, y_send, y_recv, z_send, z_recv, all_send, all_recv,
):
    n_lat, n_y, n_z = sizes
    n_lon = n_y * n_z
    lat, lon = lax.axis_index("lat"), lax.axis_index("lon")
    y, z = lon // n_z, lon % n_z
    above, below = lon - 1 + n_lon, lon + 1
    west_id, east_id = {"lon": above % n_lon}, {"lon": below % n_lon}

    def lat_peer(step):
        return (lat + step) % n_lat

    def y_peer(step):
        return (y + step) % n_y

    def z_peer(step):
        return (z + step) % n_z

    main = pl.ds(0, LANES)

    def load(c):
        return pltpu.make_async_copy(
            fields.at[c, :, :, main], body.at[c, pl.ds(0, ROWS), pl.ds(0, COLS), :], load_sem.at[c]
        )

    tail_load = pltpu.make_async_copy(
        fields.at[:, :, :, pl.ds(LANES, 1)], last, tail_sem.at[0]
    )
    edge_load = pltpu.make_async_copy(fields.at[:, :, COLS - 1, main], edge, tail_sem.at[1])
    tail_load.start()

    def start_load(c, carry):
        load(c).start()
        return carry

    lax.fori_loop(0, CHANNELS, start_load, 0)
    edge_load.start()

    barrier = pltpu.get_barrier_semaphore()
    greeted = [west_id, east_id]
    greeted += [{"lat": lat_peer(step)} for step in range(1, n_lat)]
    greeted += [{"lon": y_peer(step) * n_z + z} for step in range(1, n_y)]
    greeted += [{"lon": y * n_z + z_peer(step)} for step in range(1, n_z) if min(step, n_z - step) <= 2]
    for peer in greeted:
        pl.semaphore_signal(barrier, inc=1, device_id=peer, device_id_type=MESH)

    body[:, ROWS : ROWS + 1, 0:COLS, :] = jnp.zeros((CHANNELS, 1, COLS, LANES), F32)
    body[:, :, COLS : COLS + 8, :] = jnp.zeros((CHANNELS, ROWS + 1, 8, LANES), F32)
    acc_one[...] = jnp.zeros_like(acc_one)
    acc_two[...] = jnp.zeros_like(acc_two)

    tail_load.wait()
    wide_lane = iota((LANES, LANES), 1)
    merged = jnp.zeros((LANES, LANES), F32)
    for c in range(CHANNELS):
        for q in range(4):
            line = last[c, 4 * q : 4 * q + 4].reshape(LANES, 1)
            merged = jnp.where(wide_lane == 4 * c + q, jnp.broadcast_to(line, (LANES, LANES)), merged)
    tail_cells[...] = merged
    pack_row[...] = merged[0:COLS]
    sub8 = iota((8, LANES), 0)

    def column(ref_or_value, j):
        lines = [jnp.broadcast_to(ref_or_value[COLS * i + j : COLS * i + j + 1, :], (8, LANES)) for i in range(4)]
        result = lines[3]
        for i in range(3):
            result = jnp.where(sub8 == i, lines[i], result)
        return result

    pack_col[...] = column(tail_cells, 0)
    count = 4 * CHANNELS
    tail = merged.T[:count]
    row, lane = iota((count, LANES), 0), iota((count, LANES), 1)
    right = tail * jnp.where(lane % COLS == COLS - 1, 0.0, pltpu.roll(tail, LANES - 1, 1))
    ahead = pltpu.roll(tail, LANES - COLS, 1)
    further = jnp.where(row % 4 == 3, 0.0, pltpu.roll(ahead, count - 1, 0))
    lower = tail * jnp.where(lane < LANES - COLS, ahead, further)
    for f, values in enumerate((tail, lower, right)):
        high = values.astype(BF16).astype(F32)
        low = values - high
        for pair in range(CHANNELS // 2):
            high8, low8 = high[8 * pair : 8 * pair + 8], low[8 * pair : 8 * pair + 8]
            first = jnp.where(sub8 < 4, high8, pltpu.roll(low8, 4, 0))
            second = jnp.where(sub8 < 4, pltpu.roll(high8, 4, 0), low8)
            for c, both in ((2 * pair, first), (2 * pair + 1, second)):
                for q in range(4):
                    part_q = jnp.where(sub8 % 4 == q, both, 0.0)
                    part_q = jnp.concatenate([part_q, jnp.zeros((8, LANES), F32)], axis=0)
                    tails_ref[f, c, :, LANES * q : LANES * q + LANES] = part_q.astype(BF16)
    own_one = sums(tail, tail)
    own_two = sums(lower, lower) + sums(right, right)

    pl.semaphore_wait(barrier, len(greeted))
    relayed = n_z > 5
    if relayed:
        for step in (2, n_z - 2):
            pl.semaphore_signal(
                relay_sem, inc=1, device_id={"lon": y * n_z + z_peer(step)}, device_id_type=MESH
            )

    def remote(source, target, index, peer):
        return pltpu.make_async_remote_copy(
            source, target, halo_send.at[index], halo_recv.at[index], device_id=peer, device_id_type=MESH
        )

    lat_up = {"lat": lax.max(lat - 1, 0)}
    lat_down = {"lat": lax.min(lat + 1, n_lat - 1)}
    east_copies = [
        remote(fields.at[:, :, 0, main], east, 0, west_id),
        remote(pack_col, got_col, 1, west_id),
    ]
    south_copies = [
        remote(fields.at[:, 0, :, main], south, 2, lat_up),
        remote(pack_row, got_row, 3, lat_up),
    ]
    west_copy = remote(fields.at[:, :, COLS - 1, main], west, 4, east_id)
    north_copy = remote(fields.at[:, ROWS - 1, :, main], north, 5, lat_down)

    @pl.when(lat > 0)
    def _():
        for copy in south_copies:
            copy.start()

    for copy in east_copies:
        copy.start()

    zero = jnp.zeros((8, LANES), F32)

    def channel(c, carry):
        rest_one, rest_two = carry
        load(c).wait()
        value = body[c, 0:ROWS, 0:COLS, :]
        product, rest = self_product(flat(value), tails_ref[0, c])
        acc_one[...] += product
        rest_one += rest
        product, rest = self_product(flat(value * body[c, 1 : ROWS + 1, 0:COLS, :]), tails_ref[1, c])
        acc_two[...] += product
        rest_two += rest
        product, rest = self_product(flat(value * body[c, 0:ROWS, 1 : COLS + 1, :]), tails_ref[2, c])
        acc_two[...] += product
        rest_two += rest
        return rest_one, rest_two

    rest_one, rest_two = lax.fori_loop(0, CHANNELS, channel, (zero, zero), unroll=True)
    edge_load.wait()

    @pl.when(lat < n_lat - 1)
    def _():
        for copy in south_copies:
            copy.wait_recv()

    for copy in east_copies:
        copy.wait_recv()

    @pl.when(lat < n_lat - 1)
    def _():
        north_copy.start()

    west_copy.start()

    @pl.when(lat == n_lat - 1)
    def _():
        south[...] = jnp.zeros_like(south)
        got_row[...] = jnp.zeros_like(got_row)

    @pl.when(lat == 0)
    def _():
        north[...] = jnp.zeros_like(north)

    def spread(packed, lane):
        return jnp.broadcast_to(packed[:, lane : lane + 1], (8, LANES))

    row_pairs = pltpu.roll(tail_cells[LANES - COLS : LANES, :], LANES - 3, 1) * got_row[...]
    column_pairs = column(tail_cells, COLS - 1) * got_col[...]
    column_pairs = jnp.where(sub8 < 4, column_pairs, pltpu.roll(pltpu.roll(column_pairs, 4, 0), LANES - 1, 1))
    tails = [
        spread(row_pairs[8 * t : 8 * t + 8], 4 * c) for c in range(CHANNELS) for t in range(COLS // 8)
    ]
    tails += [spread(column_pairs, 4 * c + 2 * h) for c in range(CHANNELS) for h in range(2)]
    tails = jnp.concatenate(tails, axis=0)
    border = jnp.concatenate(
        [flat(body[:, ROWS - 1, 0:COLS, :] * south[...]), flat(edge[...] * east[...])], axis=0
    )
    product, rest = self_product(border)
    rest_two += rest
    cross_two = sums(border, tails)
    border_own = sums(tails, tails).sum(axis=0, keepdims=True)

    scale = 1.0 / cells_total
    total = (acc_one[...] + 2.0 * acc_two[...]) * scale
    rest = (rest_one + 2.0 * rest_two).sum(axis=0, keepdims=True) * scale
    square = total[:LANES] + product * (2.0 * scale)
    twisted = square[:, LANES:]
    full = square[:, :LANES] + (twisted + twisted.T)
    full += jnp.where(iota((LANES, LANES), 0) == iota((LANES, LANES), 1), rest, 0.0)
    cross = cross_two.sum(axis=0, keepdims=True) * (2.0 * scale)
    mixed = total[LANES : LANES + 8]
    mixed = mixed[:, :LANES] + jnp.where(sub8 < 4, mixed[:, LANES:], 0.0)
    cross += mixed.sum(axis=0, keepdims=True)
    own = (own_one + 2.0 * own_two).sum(axis=0, keepdims=True).sum(axis=1, keepdims=True)
    own = (jnp.broadcast_to(own, (1, LANES)) + 2.0 * border_own) * scale

    half = LANES // 2
    top, bottom = full[:half], full[half:]
    row, lane = iota((half, LANES), 0), iota((half, LANES), 1)
    folded = jnp.where((lane < half) & (row < lane), pltpu.roll(bottom, half, 1), top)
    diagonal = jnp.where(lane == row + half, bottom, 0.0).sum(axis=0, keepdims=True)
    extra = jnp.where(iota((1, LANES), 1) < half, own, diagonal)
    rows = half // n_lat
    for owner in range(n_lat):
        part[owner, 0:rows, :] = folded[owner * rows : (owner + 1) * rows]
        tail = cross if owner == 0 else extra if owner == 1 else jnp.zeros((1, LANES), F32)
        part[owner, rows : rows + 1, :] = tail

    def exchange(count, me, peer_of, device_of, source_of, buf, send, recv):
        def start(step):
            peer = peer_of(step)
            pltpu.make_async_remote_copy(
                source_of(peer), buf.at[me], send.at[0], recv.at[0], device_id=device_of(peer), device_id_type=MESH
            ).start()

        start(count // 2)

        def start_two(t, carry):
            start(count // 2 + t)
            start(count // 2 - t)
            return carry

        lax.fori_loop(1, count // 2, start_two, 0)
        others = buf.at[pl.ds(0, count - 1)]
        pltpu.make_async_copy(others, others, recv.at[0]).wait()
        return pltpu.make_async_copy(others, others, send.at[0])

    def added(buf, count):
        result = buf[0]
        for index in range(1, count):
            result = result + buf[index]
        return result

    lat_buf[lat] = part[lat]
    pending = [exchange(
        n_lat, lat, lat_peer, lambda p: {"lat": p}, lambda p: part.at[p], lat_buf, lat_send, lat_recv
    )]
    y_buf[y] = added(lat_buf, n_lat)
    pending += [exchange(
        n_y, y, y_peer, lambda p: {"lon": p * n_z + z}, lambda p: y_buf.at[y], y_buf, y_send, y_recv
    )]
    z_buf[z] = added(y_buf, n_y)
    if relayed:
        pl.semaphore_wait(relay_sem, 2)
    pending += [exchange(
        n_z, z, z_peer, lambda p: {"lon": y * n_z + p}, lambda p: z_buf.at[z], z_buf, z_send, z_recv
    )]
    all_buf[lat] = added(z_buf, n_z)
    pending += [exchange(
        n_lat, lat, lat_peer, lambda p: {"lat": p}, lambda p: all_buf.at[lat], all_buf, all_send, all_recv
    )]
    gram_out[...] = all_buf[...]

    @pl.when(lat > 0)
    def _():
        north_copy.wait_recv()
        for copy in south_copies:
            copy.wait_send()

    @pl.when(lat < n_lat - 1)
    def _():
        north_copy.wait_send()

    west_copy.wait_recv()
    for copy in [west_copy] + east_copies:
        copy.wait_send()
    for copy in pending:
        copy.wait()
    north_out[...] = north[...]
    south_out[...] = south[...]
    west_out[...] = west[...]
    east_out[...] = east[...]


def gram_call(fields, n_lat, n_lon):
    n_z = 8 if n_lon % 32 == 0 else max(n_lon // 2, 1)
    n_y = n_lon // n_z
    rows = LANES // 2 // n_lat + 1
    cells_total = 5 * CHANNELS * ROWS * n_lat * COLS * n_lon
    row_shape, col_shape = (CHANNELS, COLS, LANES), (CHANNELS, ROWS, LANES)
    chunk = (rows, LANES)
    dma = pltpu.SemaphoreType.DMA
    shapes = [(n_lat,) + chunk, row_shape, row_shape, col_shape, col_shape]
    vmem = pl.BlockSpec(memory_space=pltpu.VMEM)
    return pl.pallas_call(
        functools.partial(gram_kernel, (n_lat, n_y, n_z), cells_total),
        out_shape=[jax.ShapeDtypeStruct(shape, F32) for shape in shapes],
        in_specs=[pl.BlockSpec(memory_space=pltpu.HBM)],
        out_specs=[vmem] * 5,
        scratch_shapes=[
            pltpu.VMEM((CHANNELS, ROWS + 1, COLS + 8, LANES), F32),
            pltpu.VMEM((CHANNELS, ROWS, COLS, 1), F32),
            pltpu.VMEM(col_shape, F32),
            pltpu.VMEM(row_shape, F32),
            pltpu.VMEM(row_shape, F32),
            pltpu.VMEM(col_shape, F32),
            pltpu.VMEM(col_shape, F32),
        ]
        + [pltpu.VMEM((COLS, LANES), F32), pltpu.VMEM((8, LANES), F32)] * 2
        + [pltpu.VMEM((LANES, LANES), F32), pltpu.VMEM((3, CHANNELS, 16, 4 * LANES), BF16)]
        + [pltpu.VMEM((LANES + 16, 2 * LANES), F32)] * 2
        + [
            pltpu.VMEM((n_lat,) + chunk, F32),
            pltpu.VMEM((n_lat,) + chunk, F32),
            pltpu.VMEM((n_y,) + chunk, F32),
            pltpu.VMEM((n_z,) + chunk, F32),
            pltpu.VMEM((n_lat,) + chunk, F32),
            pltpu.SemaphoreType.REGULAR,
            dma((CHANNELS,)), dma((2,)),
            dma((6,)), dma((6,)),
            dma((1,)), dma((1,)),
            dma((1,)), dma((1,)),
            dma((1,)), dma((1,)),
            dma((1,)), dma((1,)),
        ],
        compiler_params=pltpu.CompilerParams(
            collective_id=0, has_side_effects=True, vmem_limit_bytes=48 << 20
        ),
    )(fields)


def unfolded(gram):
    n_lat, rows, _ = gram.shape
    half = LANES // 2
    folded = jnp.concatenate([gram[owner, : rows - 1, :] for owner in range(n_lat)], axis=0)
    cross, extra = gram[0, rows - 1 : rows, :], gram[1, rows - 1 : rows, :]
    row, lane = iota((half, LANES), 0), iota((half, LANES), 1)
    top = jnp.where((lane < half) & (row <= lane), 0.0, folded)
    bottom = jnp.where((lane >= half) & (row < lane - half), pltpu.roll(folded, half, 1), 0.0)
    once = jnp.concatenate([top, bottom], axis=0)
    diagonal = jnp.concatenate(
        [jnp.where(lane == row, folded, 0.0), jnp.where(lane == row + half, jnp.broadcast_to(extra, (half, LANES)), 0.0)],
        axis=0,
    )
    full = once + once.T + diagonal
    row, lane = iota((LANES, LANES), 0), iota((LANES, LANES), 1)

    def column(line):
        return jnp.where(row == lane, jnp.broadcast_to(line, (LANES, LANES)), 0.0).sum(axis=1, keepdims=True)

    corner = extra[:, 0:1]
    shifted = pltpu.roll(pltpu.roll(full, LANES - 1, 0), LANES - 1, 1)
    line = jnp.where(iota((1, LANES), 1) == LANES - 1, corner, pltpu.roll(cross, LANES - 1, 1))
    shifted = jnp.where(lane == LANES - 1, column(line), shifted)
    shifted = jnp.where(row == LANES - 1, jnp.broadcast_to(line, (LANES, LANES)), shifted)
    identity = jnp.where(row == lane, 1.0, 0.0)
    first = jnp.where(lane == LANES - 1, column(cross), identity)
    low = jnp.where(row == LANES - 1, cross[:, 0:1], pltpu.roll(full, LANES - 1, 0)[:, 0:1])
    second = jnp.where(lane == LANES - 1, low, identity)
    return (full, first), (shifted, second)


def split_three(value):
    one = value.astype(BF16).astype(F32)
    two = (value - one).astype(BF16).astype(F32)
    return one, two, value - one - two


def eliminate(b, works, splats, nears, turned_refs, done_refs, first_row):
    start = b * 8
    sub, lane = iota((8, LANES), 0), iota((8, LANES), 1)
    upper = sub < 4
    left_part, right_part = slice(0, LANES), slice(LANES, 2 * LANES)
    after = lax.min(b + 1, LANES // 8 - 1)

    def joined(first, second):
        return [jnp.where(upper, first, pltpu.roll(second, 4, 0)), jnp.where(upper, pltpu.roll(first, 4, 0), second)]

    following = []
    for work, turned, done in zip(works, turned_refs, done_refs):
        small = jnp.dot(turned[after].astype(BF16), done[...], preferred_element_type=F32)
        following.append(work[after] - small)
    below = slice(first_row // 8, LANES // 8)
    for work, turned, done in zip(works, turned_refs, done_refs):
        update = jnp.dot(flat(turned[below]).astype(BF16), done[...], preferred_element_type=F32)
        work[below] = work[below] - update.reshape(-1, 8, 2 * LANES)
    next_left = joined(*[rows[:, left_part] for rows in following])
    next_right = joined(*[rows[:, right_part] for rows in following])

    shift = (LANES - start) % LANES

    def columns_of(rows, first):
        block = pltpu.roll(rows, shift, 1)
        return {j: jnp.broadcast_to(block[:, j : j + 1], (8, LANES)) for j in range(first, 8)}

    for h in range(2):
        for j, column in columns_of(nears[h, :, left_part], 4 * h).items():
            splats[h, j] = column

    def paired(ref, row):
        first, second = ref[row : row + 1, :], ref[4 + row : 5 + row, :]
        return jnp.where(upper, jnp.broadcast_to(first, (8, LANES)), jnp.broadcast_to(second, (8, LANES)))

    entry = {}
    for i in range(8):
        for j in range(i, 8):
            entry[i, j] = paired(splats.at[i // 4, j], i % 4)
    left_rows = [paired(nears.at[i // 4, :, left_part], i % 4) for i in range(8)]
    right_rows = [paired(nears.at[i // 4, :, right_part], i % 4) for i in range(8)]
    next_columns = [columns_of(rows, 0) for rows in next_left]
    inverse = []
    for k in range(8):
        inverse.append(1.0 / entry[k, k])
        for i in range(k + 1, 8):
            factor = entry[k, i] * inverse[k]
            for j in range(i, 8):
                entry[i, j] = entry[i, j] - factor * entry[k, j]
            left_rows[i] = left_rows[i] - factor * left_rows[k]
            right_rows[i] = right_rows[i] - factor * right_rows[k]
        for h in range(2):
            factor = next_columns[h][k] * inverse[k]
            for j in range(k + 1, 8):
                next_columns[h][j] = next_columns[h][j] - factor * entry[k, j]
            next_left[h] = next_left[h] - factor * left_rows[k]
            next_right[h] = next_right[h] - factor * right_rows[k]
    for h in range(2):
        nears[h, :, left_part] = next_left[h]
        nears[h, :, right_part] = next_right[h]

    def gathered(rows):
        low, high = rows[0], rows[4]
        for k in range(1, 4):
            low = jnp.where(sub % 4 == k, rows[k], low)
            high = jnp.where(sub % 4 == k, rows[4 + k], high)
        return joined(low, high)

    for work, turned, done, pivots, done_left, done_right in zip(
        works, turned_refs, done_refs, gathered(inverse), gathered(left_rows), gathered(right_rows)
    ):
        f1, f2, f3 = split_three(jnp.where(lane >= start + 16, done_left * pivots, 0.0))
        d1, d2, d3 = split_three(jnp.concatenate([done_left, done_right], axis=1))
        turned[...] = jnp.concatenate([f1, f1, f2, f1, f2, f3], axis=0).T.reshape(-1, 8, 48)
        done[...] = jnp.concatenate([d1, d2, d1, d3, d2, d1], axis=0).astype(BF16)
        root = jnp.sqrt(pivots)
        work[b, :, left_part] = done_left * root
        work[b, :, right_part] = done_right * root


def accurate(left, right):
    return lax.dot_general(
        left, right, (((1,), (1,)), ((), ())), precision=lax.Precision.HIGHEST, preferred_element_type=F32
    )


def modes_kernel(
    fields, gram, north, south, west, east, modes, forward, backward,
    body, work_one, work_two, splat, near, turned_one, turned_two, done_one, done_two, weights, first_column, plain, lower, left, right, operators,
    load_sem, store_sem,
):
    works, turned, done = (work_one, work_two), (turned_one, turned_two), (done_one, done_two)
    main = pl.ds(0, LANES)
    inner = pl.ds(1, ROWS)
    loads = [
        pltpu.make_async_copy(fields.at[:, :, :, main], body.at[:, inner, pl.ds(0, COLS), :], load_sem.at[0]),
        pltpu.make_async_copy(north, body.at[:, 0, pl.ds(0, COLS), :], load_sem.at[1]),
        pltpu.make_async_copy(south, body.at[:, ROWS + 1, pl.ds(0, COLS), :], load_sem.at[2]),
        pltpu.make_async_copy(fields.at[:, :, 0, main], first_column, load_sem.at[3]),
        pltpu.make_async_copy(east, body.at[:, inner, COLS, :], load_sem.at[4]),
    ]
    for copy in loads:
        copy.start()

    for work, (matrix, extended) in zip(works, unfolded(gram[...])):
        work[:, :, 0:LANES] = matrix.reshape(-1, 8, LANES)
        work[:, :, LANES : 2 * LANES] = extended.reshape(-1, 8, LANES)

    upper = iota((8, LANES), 0) < 4
    for part in range(0, 2 * LANES, LANES):
        first, second = [work[0, :, part : part + LANES] for work in works]
        near[0, :, part : part + LANES] = jnp.where(upper, first, pltpu.roll(second, 4, 0))
        near[1, :, part : part + LANES] = jnp.where(upper, pltpu.roll(first, 4, 0), second)
    for ref in turned + done:
        ref[...] = jnp.zeros_like(ref)

    for phase in range(4):

        def step(b, carry):
            eliminate(b, works, splat, near, turned, done, phase * 32)
            return carry

        lax.fori_loop(phase * 4, phase * 4 + 4, step, 0)

    row, lane = iota((LANES, LANES), 0), iota((LANES, LANES), 1)

    def parts(c):
        factor, extended = flat(works[c][:, :, 0:LANES]), flat(works[c][:, :, LANES : 2 * LANES])
        corner = jnp.where((row == LANES - 1) & (lane == LANES - 1), 1.0 / factor, 0.0)
        return factor, extended, jnp.where(lane == LANES - 1, corner, extended)

    factor, extended, inverse = parts(0)
    mixing = inverse.T
    high = mixing.astype(BF16)
    low = (mixing - high.astype(F32)).astype(BF16)
    line = jnp.concatenate([high, low], axis=1)
    weights[...] = jnp.concatenate([line, line], axis=0)

    for copy in loads:
        copy.wait()

    def mixed(value):
        both = jnp.dot(split_pair(value), weights[...], preferred_element_type=F32)
        return both[:, :LANES] + both[:, LANES:]

    inner_cols, outer_cols = pl.ds(0, COLS - 1), pl.ds(1, COLS - 1)

    def stores(c):
        pieces = (
            (plain.at[c], modes.at[c]),
            (lower.at[c, pl.ds(0, ROWS)], modes.at[CHANNELS + c]),
            (lower.at[c, pl.ds(1, ROWS)], modes.at[2 * CHANNELS + c]),
            (right.at[c, :, inner_cols, :], modes.at[3 * CHANNELS + c, :, outer_cols, :]),
            (right.at[c], modes.at[4 * CHANNELS + c]),
        )
        return [pltpu.make_async_copy(*piece, store_sem.at[kind]) for kind, piece in enumerate(pieces)]

    def stored(kind):
        whole = modes.at[pl.ds(kind * CHANNELS, CHANNELS)]
        if kind == 3:
            whole = whole.at[:, :, outer_cols, :]
        return pltpu.make_async_copy(whole, whole, store_sem.at[kind])

    first_store = pltpu.make_async_copy(
        left, modes.at[pl.ds(3 * CHANNELS, CHANNELS), :, 0, :], load_sem.at[0]
    )
    left[...] = mixed(flat(first_column[...] * west[...])).reshape((CHANNELS, ROWS, LANES))
    first_store.start()

    def channel(c, carry):
        value = body[c, 1 : ROWS + 1, 0:COLS, :]
        pairs = body[c, 0 : ROWS + 1, 0:COLS, :] * body[c, 1 : ROWS + 2, 0:COLS, :]
        beside = value * body[c, 1 : ROWS + 1, 1 : COLS + 1, :]
        both = mixed(jnp.concatenate([flat(value), flat(pairs), flat(beside)], axis=0))
        cells = ROWS * COLS
        plain[c] = both[:cells].reshape((ROWS, COLS, LANES))
        lower[c] = both[cells : 2 * cells + COLS].reshape((ROWS + 1, COLS, LANES))
        right[c] = both[2 * cells + COLS :].reshape((ROWS, COLS, LANES))
        for copy in stores(c):
            copy.start()
        return carry

    lax.fori_loop(0, CHANNELS, channel, 0, unroll=True)

    shifted = jnp.where(lane == LANES - 1, extended, pltpu.roll(factor, LANES - 1, 1))
    operators[0] = accurate(shifted, inverse)
    forward_store = pltpu.make_async_copy(operators.at[0], forward, load_sem.at[1])
    forward_store.start()
    factor, extended, inverse = parts(1)
    mixed_block = jnp.where(lane == 0, pltpu.roll(extended, 1, 1), pltpu.roll(factor, 1, 1))
    operators[1] = accurate(mixed_block, inverse)
    backward_store = pltpu.make_async_copy(operators.at[1], backward, load_sem.at[2])
    backward_store.start()
    for kind in range(5):
        stored(kind).wait()
    first_store.wait()
    forward_store.wait()
    backward_store.wait()


def modes_call(fields, gram, north, south, west, east):
    shape = (CHANNELS, ROWS, COLS, LANES)
    any_space = pl.BlockSpec(memory_space=pl.ANY)
    vmem = pl.BlockSpec(memory_space=pltpu.VMEM)
    return pl.pallas_call(
        modes_kernel,
        out_shape=[
            jax.ShapeDtypeStruct((5 * CHANNELS, ROWS, COLS, LANES), F32),
            jax.ShapeDtypeStruct((LANES, LANES), F32),
            jax.ShapeDtypeStruct((LANES, LANES), F32),
        ],
        in_specs=[pl.BlockSpec(memory_space=pltpu.HBM), vmem, any_space, any_space, vmem, any_space],
        out_specs=[any_space] * 3,
        scratch_shapes=[
            pltpu.VMEM((CHANNELS, ROWS + 2, COLS + 8, LANES), F32),
            pltpu.VMEM((LANES // 8, 8, 2 * LANES), F32),
            pltpu.VMEM((LANES // 8, 8, 2 * LANES), F32),
            pltpu.VMEM((2, 8, 8, LANES), F32),
            pltpu.VMEM((2, 8, 2 * LANES), F32),
            pltpu.VMEM((LANES // 8, 8, 48), F32),
            pltpu.VMEM((LANES // 8, 8, 48), F32),
            pltpu.VMEM((48, 2 * LANES), BF16),
            pltpu.VMEM((48, 2 * LANES), BF16),
            pltpu.VMEM((2 * LANES, 2 * LANES), BF16),
            pltpu.VMEM((CHANNELS, ROWS, LANES), F32),
            pltpu.VMEM(shape, F32),
            pltpu.VMEM((CHANNELS, ROWS + 1, COLS, LANES), F32),
            pltpu.VMEM((CHANNELS, ROWS, LANES), F32),
            pltpu.VMEM(shape, F32),
            pltpu.VMEM((2, LANES, LANES), F32),
            pltpu.SemaphoreType.DMA((5,)),
            pltpu.SemaphoreType.DMA((5,)),
        ],
        compiler_params=pltpu.CompilerParams(vmem_limit_bytes=48 << 20),
    )(fields, gram, north, south, west, east)


def shards(fields):
    cells = pltpu.with_memory_space_constraint(fields.transpose(1, 2, 3, 0), pltpu.HBM)
    gram, north, south, west, east = gram_call(cells, lax.axis_size("lat"), lax.axis_size("lon"))
    return tuple(modes_call(cells, gram, north, south, west, east))


def solution(mesh):
    return jax.shard_map(
        shards,
        mesh=mesh,
        in_specs=(P(None, None, "lat", "lon"),),
        out_specs=(P(None, "lat", "lon", None), P(), P()),
        check_vma=False,
    )
```

```python
import functools

import jax
import jax.numpy as jnp
from jax import lax
from jax.experimental import pallas as pl
from jax.experimental.pallas import tpu as pltpu
from jax.sharding import PartitionSpec as P

F32, BF16 = jnp.float32, jnp.bfloat16
MESH = pl.DeviceIdType.MESH
CHANNELS, ROWS, COLS, LANES = 6, 16, 32, 128


def split_pair(value):
    high = value.astype(BF16)
    low = (value - high.astype(F32)).astype(BF16)
    return jnp.concatenate([high, low], axis=-1)


def flat(value):
    return value.reshape(-1, value.shape[-1])


def iota(shape, dim):
    return lax.broadcasted_iota(jnp.int32, shape, dim)


def sums(value, other):
    return (value * other).reshape(-1, 8, LANES).sum(axis=0)


def self_product(value, tails=None):
    high = value.astype(BF16)
    rest = value - high.astype(F32)
    pair = jnp.concatenate([high, rest.astype(BF16)], axis=-1)
    turned = high.T
    squares = pair[:, LANES:] * pair[:, LANES:]
    squares = squares.reshape(-1, 16, LANES)
    count = squares.shape[0]
    total = jnp.zeros((8, LANES), F32)
    for first in range(0, count, 8):
        group = [squares[index] for index in range(first, min(first + 8, count))]
        while len(group) > 1:
            group = [left + right for left, right in zip(group[::2], group[1::2])] + group[len(group) // 2 * 2 :]
        total += group[0].astype(F32).reshape(2, 8, LANES).sum(axis=0)
    if tails is not None:
        turned = jnp.concatenate([turned, tails], axis=0)
    return jnp.dot(turned, pair, preferred_element_type=F32), total


def gram_kernel(
    sizes, cells_total, fields,
    gram_out, north_out, south_out, west_out, east_out,
    body, last, edge, north, south, west, east,
    pack_row, pack_col, got_row, got_col, tail_cells, tails_ref,
    acc_one, acc_two, part, lat_buf, y_buf, z_buf, all_buf,
    relay_sem, load_sem, tail_sem, halo_send, halo_recv, lat_send, lat_recv, y_send, y_recv, z_send, z_recv, all_send, all_recv,
):
    n_lat, n_y, n_z = sizes
    n_lon = n_y * n_z
    lat, lon = lax.axis_index("lat"), lax.axis_index("lon")
    y, z = lon // n_z, lon % n_z
    above, below = lon - 1 + n_lon, lon + 1
    west_id, east_id = {"lon": above % n_lon}, {"lon": below % n_lon}

    def lat_peer(step):
        return (lat + step) % n_lat

    def y_peer(step):
        return (y + step) % n_y

    def z_peer(step):
        return (z + step) % n_z

    main = pl.ds(0, LANES)

    def load(c):
        return pltpu.make_async_copy(
            fields.at[c, :, :, main], body.at[c, pl.ds(0, ROWS), pl.ds(0, COLS), :], load_sem.at[c]
        )

    tail_load = pltpu.make_async_copy(
        fields.at[:, :, :, pl.ds(LANES, 1)], last, tail_sem.at[0]
    )
    edge_load = pltpu.make_async_copy(fields.at[:, :, COLS - 1, main], edge, tail_sem.at[1])
    tail_load.start()

    def start_load(c, carry):
        load(c).start()
        return carry

    lax.fori_loop(0, CHANNELS, start_load, 0)
    edge_load.start()

    barrier = pltpu.get_barrier_semaphore()
    greeted = [west_id, east_id]
    greeted += [{"lat": lat_peer(step)} for step in range(1, n_lat)]
    greeted += [{"lon": y_peer(step) * n_z + z} for step in range(1, n_y)]
    greeted += [{"lon": y * n_z + z_peer(step)} for step in range(1, n_z) if min(step, n_z - step) <= 2]
    for peer in greeted:
        pl.semaphore_signal(barrier, inc=1, device_id=peer, device_id_type=MESH)

    body[:, ROWS : ROWS + 1, 0:COLS, :] = jnp.zeros((CHANNELS, 1, COLS, LANES), F32)
    body[:, :, COLS : COLS + 8, :] = jnp.zeros((CHANNELS, ROWS + 1, 8, LANES), F32)
    acc_one[...] = jnp.zeros_like(acc_one)
    acc_two[...] = jnp.zeros_like(acc_two)

    tail_load.wait()
    wide_lane = iota((LANES, LANES), 1)
    merged = jnp.zeros((LANES, LANES), F32)
    for c in range(CHANNELS):
        for q in range(4):
            line = last[c, 4 * q : 4 * q + 4].reshape(LANES, 1)
            merged = jnp.where(wide_lane == 4 * c + q, jnp.broadcast_to(line, (LANES, LANES)), merged)
    tail_cells[...] = merged
    pack_row[...] = merged[0:COLS]
    sub8 = iota((8, LANES), 0)

    def column(ref_or_value, j):
        lines = [jnp.broadcast_to(ref_or_value[COLS * i + j : COLS * i + j + 1, :], (8, LANES)) for i in range(4)]
        result = lines[3]
        for i in range(3):
            result = jnp.where(sub8 == i, lines[i], result)
        return result

    pack_col[...] = column(tail_cells, 0)
    count = 4 * CHANNELS
    tail = merged.T[:count]
    row, lane = iota((count, LANES), 0), iota((count, LANES), 1)
    right = tail * jnp.where(lane % COLS == COLS - 1, 0.0, pltpu.roll(tail, LANES - 1, 1))
    ahead = pltpu.roll(tail, LANES - COLS, 1)
    further = jnp.where(row % 4 == 3, 0.0, pltpu.roll(ahead, count - 1, 0))
    lower = tail * jnp.where(lane < LANES - COLS, ahead, further)
    for f, values in enumerate((tail, lower, right)):
        high = values.astype(BF16).astype(F32)
        low = values - high
        for pair in range(CHANNELS // 2):
            high8, low8 = high[8 * pair : 8 * pair + 8], low[8 * pair : 8 * pair + 8]
            first = jnp.where(sub8 < 4, high8, pltpu.roll(low8, 4, 0))
            second = jnp.where(sub8 < 4, pltpu.roll(high8, 4, 0), low8)
            for c, both in ((2 * pair, first), (2 * pair + 1, second)):
                for q in range(4):
                    part_q = jnp.where(sub8 % 4 == q, both, 0.0)
                    part_q = jnp.concatenate([part_q, jnp.zeros((8, LANES), F32)], axis=0)
                    tails_ref[f, c, :, LANES * q : LANES * q + LANES] = part_q.astype(BF16)
    own_one = sums(tail, tail)
    own_two = sums(lower, lower) + sums(right, right)

    pl.semaphore_wait(barrier, len(greeted))
    relayed = n_z > 5
    if relayed:
        for step in (2, n_z - 2):
            pl.semaphore_signal(
                relay_sem, inc=1, device_id={"lon": y * n_z + z_peer(step)}, device_id_type=MESH
            )

    def remote(source, target, index, peer):
        return pltpu.make_async_remote_copy(
            source, target, halo_send.at[index], halo_recv.at[index], device_id=peer, device_id_type=MESH
        )

    lat_up = {"lat": lax.max(lat - 1, 0)}
    lat_down = {"lat": lax.min(lat + 1, n_lat - 1)}
    east_copies = [
        remote(fields.at[:, :, 0, main], east, 0, west_id),
        remote(pack_col, got_col, 1, west_id),
    ]
    south_copies = [
        remote(fields.at[:, 0, :, main], south, 2, lat_up),
        remote(pack_row, got_row, 3, lat_up),
    ]
    west_copy = remote(fields.at[:, :, COLS - 1, main], west, 4, east_id)
    north_copy = remote(fields.at[:, ROWS - 1, :, main], north, 5, lat_down)

    @pl.when(lat > 0)
    def _():
        for copy in south_copies:
            copy.start()

    for copy in east_copies:
        copy.start()

    zero = jnp.zeros((8, LANES), F32)

    def channel(c, carry):
        rest_one, rest_two = carry
        load(c).wait()
        value = body[c, 0:ROWS, 0:COLS, :]
        product, rest = self_product(flat(value), tails_ref[0, c])
        acc_one[...] += product
        rest_one += rest
        product, rest = self_product(flat(value * body[c, 1 : ROWS + 1, 0:COLS, :]), tails_ref[1, c])
        acc_two[...] += product
        rest_two += rest
        product, rest = self_product(flat(value * body[c, 0:ROWS, 1 : COLS + 1, :]), tails_ref[2, c])
        acc_two[...] += product
        rest_two += rest
        return rest_one, rest_two

    rest_one, rest_two = lax.fori_loop(0, CHANNELS, channel, (zero, zero), unroll=True)
    edge_load.wait()

    @pl.when(lat < n_lat - 1)
    def _():
        for copy in south_copies:
            copy.wait_recv()

    for copy in east_copies:
        copy.wait_recv()

    @pl.when(lat < n_lat - 1)
    def _():
        north_copy.start()

    west_copy.start()

    @pl.when(lat == n_lat - 1)
    def _():
        south[...] = jnp.zeros_like(south)
        got_row[...] = jnp.zeros_like(got_row)

    @pl.when(lat == 0)
    def _():
        north[...] = jnp.zeros_like(north)

    def spread(packed, lane):
        return jnp.broadcast_to(packed[:, lane : lane + 1], (8, LANES))

    row_pairs = pltpu.roll(tail_cells[LANES - COLS : LANES, :], LANES - 3, 1) * got_row[...]
    column_pairs = column(tail_cells, COLS - 1) * got_col[...]
    column_pairs = jnp.where(sub8 < 4, column_pairs, pltpu.roll(pltpu.roll(column_pairs, 4, 0), LANES - 1, 1))
    tails = [
        spread(row_pairs[8 * t : 8 * t + 8], 4 * c) for c in range(CHANNELS) for t in range(COLS // 8)
    ]
    tails += [spread(column_pairs, 4 * c + 2 * h) for c in range(CHANNELS) for h in range(2)]
    tails = jnp.concatenate(tails, axis=0)
    border = jnp.concatenate(
        [flat(body[:, ROWS - 1, 0:COLS, :] * south[...]), flat(edge[...] * east[...])], axis=0
    )
    product, rest = self_product(border)
    rest_two += rest
    cross_two = sums(border, tails)
    border_own = sums(tails, tails).sum(axis=0, keepdims=True)

    scale = 1.0 / cells_total
    total = (acc_one[...] + 2.0 * acc_two[...]) * scale
    rest = (rest_one + 2.0 * rest_two).sum(axis=0, keepdims=True) * scale
    square = total[:LANES] + product * (2.0 * scale)
    twisted = square[:, LANES:]
    full = square[:, :LANES] + (twisted + twisted.T)
    full += jnp.where(iota((LANES, LANES), 0) == iota((LANES, LANES), 1), rest, 0.0)
    cross = cross_two.sum(axis=0, keepdims=True) * (2.0 * scale)
    mixed = total[LANES : LANES + 8]
    mixed = mixed[:, :LANES] + jnp.where(sub8 < 4, mixed[:, LANES:], 0.0)
    cross += mixed.sum(axis=0, keepdims=True)
    own = (own_one + 2.0 * own_two).sum(axis=0, keepdims=True).sum(axis=1, keepdims=True)
    own = (jnp.broadcast_to(own, (1, LANES)) + 2.0 * border_own) * scale

    half = LANES // 2
    top, bottom = full[:half], full[half:]
    row, lane = iota((half, LANES), 0), iota((half, LANES), 1)
    folded = jnp.where((lane < half) & (row < lane), pltpu.roll(bottom, half, 1), top)
    diagonal = jnp.where(lane == row + half, bottom, 0.0).sum(axis=0, keepdims=True)
    extra = jnp.where(iota((1, LANES), 1) < half, own, diagonal)
    rows = half // n_lat
    for owner in range(n_lat):
        part[owner, 0:rows, :] = folded[owner * rows : (owner + 1) * rows]
        tail = cross if owner == 0 else extra if owner == 1 else jnp.zeros((1, LANES), F32)
        part[owner, rows : rows + 1, :] = tail

    def exchange(count, me, peer_of, device_of, source_of, buf, send, recv, meanwhile=None):
        def start(step):
            peer = peer_of(step)
            pltpu.make_async_remote_copy(
                source_of(peer), buf.at[me], send.at[0], recv.at[0], device_id=device_of(peer), device_id_type=MESH
            ).start()

        start(count // 2)

        def start_two(t, carry):
            start(count // 2 + t)
            start(count // 2 - t)
            return carry

        lax.fori_loop(1, count // 2, start_two, 0)
        if meanwhile is not None:
            meanwhile()
        others = buf.at[pl.ds(0, count - 1)]
        pltpu.make_async_copy(others, others, recv.at[0]).wait()
        return pltpu.make_async_copy(others, others, send.at[0])

    def added(buf, count):
        result = buf[0]
        for index in range(1, count):
            result = result + buf[index]
        return result

    def finish_borders():
        @pl.when(lat > 0)
        def _():
            north_copy.wait_recv()
            for copy in south_copies:
                copy.wait_send()

        @pl.when(lat < n_lat - 1)
        def _():
            north_copy.wait_send()

        west_copy.wait_recv()
        for copy in [west_copy] + east_copies:
            copy.wait_send()
        north_out[...] = north[...]
        south_out[...] = south[...]
        west_out[...] = west[...]
        east_out[...] = east[...]

    lat_buf[lat] = part[lat]
    pending = [exchange(
        n_lat, lat, lat_peer, lambda p: {"lat": p}, lambda p: part.at[p], lat_buf, lat_send, lat_recv
    )]
    y_buf[y] = added(lat_buf, n_lat)
    pending += [exchange(
        n_y, y, y_peer, lambda p: {"lon": p * n_z + z}, lambda p: y_buf.at[y], y_buf, y_send, y_recv
    )]
    z_buf[z] = added(y_buf, n_y)
    if relayed:
        pl.semaphore_wait(relay_sem, 2)
    pending += [exchange(
        n_z, z, z_peer, lambda p: {"lon": y * n_z + p}, lambda p: z_buf.at[z], z_buf, z_send, z_recv
    )]
    all_buf[lat] = added(z_buf, n_z)
    pending += [exchange(
        n_lat, lat, lat_peer, lambda p: {"lat": p}, lambda p: all_buf.at[lat], all_buf, all_send, all_recv,
        finish_borders,
    )]
    gram_out[...] = all_buf[...]

    for copy in pending:
        copy.wait()


def gram_call(fields, n_lat, n_lon):
    n_z = 8 if n_lon % 32 == 0 else max(n_lon // 2, 1)
    n_y = n_lon // n_z
    rows = LANES // 2 // n_lat + 1
    cells_total = 5 * CHANNELS * ROWS * n_lat * COLS * n_lon
    row_shape, col_shape = (CHANNELS, COLS, LANES), (CHANNELS, ROWS, LANES)
    chunk = (rows, LANES)
    dma = pltpu.SemaphoreType.DMA
    shapes = [(n_lat,) + chunk, row_shape, row_shape, col_shape, col_shape]
    vmem = pl.BlockSpec(memory_space=pltpu.VMEM)
    return pl.pallas_call(
        functools.partial(gram_kernel, (n_lat, n_y, n_z), cells_total),
        out_shape=[jax.ShapeDtypeStruct(shape, F32) for shape in shapes],
        in_specs=[pl.BlockSpec(memory_space=pltpu.HBM)],
        out_specs=[vmem] * 5,
        scratch_shapes=[
            pltpu.VMEM((CHANNELS, ROWS + 1, COLS + 8, LANES), F32),
            pltpu.VMEM((CHANNELS, ROWS, COLS, 1), F32),
            pltpu.VMEM(col_shape, F32),
            pltpu.VMEM(row_shape, F32),
            pltpu.VMEM(row_shape, F32),
            pltpu.VMEM(col_shape, F32),
            pltpu.VMEM(col_shape, F32),
        ]
        + [pltpu.VMEM((COLS, LANES), F32), pltpu.VMEM((8, LANES), F32)] * 2
        + [pltpu.VMEM((LANES, LANES), F32), pltpu.VMEM((3, CHANNELS, 16, 4 * LANES), BF16)]
        + [pltpu.VMEM((LANES + 16, 2 * LANES), F32)] * 2
        + [
            pltpu.VMEM((n_lat,) + chunk, F32),
            pltpu.VMEM((n_lat,) + chunk, F32),
            pltpu.VMEM((n_y,) + chunk, F32),
            pltpu.VMEM((n_z,) + chunk, F32),
            pltpu.VMEM((n_lat,) + chunk, F32),
            pltpu.SemaphoreType.REGULAR,
            dma((CHANNELS,)), dma((2,)),
            dma((6,)), dma((6,)),
            dma((1,)), dma((1,)),
            dma((1,)), dma((1,)),
            dma((1,)), dma((1,)),
            dma((1,)), dma((1,)),
        ],
        compiler_params=pltpu.CompilerParams(
            collective_id=0, has_side_effects=True, vmem_limit_bytes=48 << 20
        ),
    )(fields)


def unfolded(gram):
    n_lat, rows, _ = gram.shape
    half = LANES // 2
    folded = jnp.concatenate([gram[owner, : rows - 1, :] for owner in range(n_lat)], axis=0)
    cross, extra = gram[0, rows - 1 : rows, :], gram[1, rows - 1 : rows, :]
    row, lane = iota((half, LANES), 0), iota((half, LANES), 1)
    top = jnp.where((lane < half) & (row <= lane), 0.0, folded)
    bottom = jnp.where((lane >= half) & (row < lane - half), pltpu.roll(folded, half, 1), 0.0)
    once = jnp.concatenate([top, bottom], axis=0)
    diagonal = jnp.concatenate(
        [jnp.where(lane == row, folded, 0.0), jnp.where(lane == row + half, jnp.broadcast_to(extra, (half, LANES)), 0.0)],
        axis=0,
    )
    full = once + once.T + diagonal
    row, lane = iota((LANES, LANES), 0), iota((LANES, LANES), 1)

    def column(line):
        return jnp.where(row == lane, jnp.broadcast_to(line, (LANES, LANES)), 0.0).sum(axis=1, keepdims=True)

    corner = extra[:, 0:1]
    shifted = pltpu.roll(pltpu.roll(full, LANES - 1, 0), LANES - 1, 1)
    line = jnp.where(iota((1, LANES), 1) == LANES - 1, corner, pltpu.roll(cross, LANES - 1, 1))
    shifted = jnp.where(lane == LANES - 1, column(line), shifted)
    shifted = jnp.where(row == LANES - 1, jnp.broadcast_to(line, (LANES, LANES)), shifted)
    identity = jnp.where(row == lane, 1.0, 0.0)
    first = jnp.where(lane == LANES - 1, column(cross), identity)
    low = jnp.where(row == LANES - 1, cross[:, 0:1], pltpu.roll(full, LANES - 1, 0)[:, 0:1])
    second = jnp.where(lane == LANES - 1, low, identity)
    return (full, first), (shifted, second)


def split_three(value):
    one = value.astype(BF16).astype(F32)
    two = (value - one).astype(BF16).astype(F32)
    return one, two, value - one - two


def eliminate(b, works, splats, nears, turned_refs, done_refs, first_row):
    start = b * 8
    sub, lane = iota((8, LANES), 0), iota((8, LANES), 1)
    upper = sub < 4
    left_part, right_part = slice(0, LANES), slice(LANES, 2 * LANES)
    after = lax.min(b + 1, LANES // 8 - 1)

    def joined(first, second):
        return [jnp.where(upper, first, pltpu.roll(second, 4, 0)), jnp.where(upper, pltpu.roll(first, 4, 0), second)]

    following = []
    for work, turned, done in zip(works, turned_refs, done_refs):
        small = jnp.dot(turned[after].astype(BF16), done[...], preferred_element_type=F32)
        following.append(work[after] - small)
    below = slice(first_row // 8, LANES // 8)
    for work, turned, done in zip(works, turned_refs, done_refs):
        update = jnp.dot(flat(turned[below]).astype(BF16), done[...], preferred_element_type=F32)
        work[below] = work[below] - update.reshape(-1, 8, 2 * LANES)
    next_left = joined(*[rows[:, left_part] for rows in following])
    next_right = joined(*[rows[:, right_part] for rows in following])

    shift = (LANES - start) % LANES

    def columns_of(rows, first):
        block = pltpu.roll(rows, shift, 1)
        return {j: jnp.broadcast_to(block[:, j : j + 1], (8, LANES)) for j in range(first, 8)}

    for h in range(2):
        for j, column in columns_of(nears[h, :, left_part], 4 * h).items():
            splats[h, j] = column

    def paired(ref, row):
        first, second = ref[row : row + 1, :], ref[4 + row : 5 + row, :]
        return jnp.where(upper, jnp.broadcast_to(first, (8, LANES)), jnp.broadcast_to(second, (8, LANES)))

    entry = {}
    for i in range(8):
        for j in range(i, 8):
            entry[i, j] = paired(splats.at[i // 4, j], i % 4)
    left_rows = [paired(nears.at[i // 4, :, left_part], i % 4) for i in range(8)]
    right_rows = [paired(nears.at[i // 4, :, right_part], i % 4) for i in range(8)]
    next_columns = [columns_of(rows, 0) for rows in next_left]
    inverse = []
    for k in range(8):
        inverse.append(1.0 / entry[k, k])
        for i in range(k + 1, 8):
            factor = entry[k, i] * inverse[k]
            for j in range(i, 8):
                entry[i, j] = entry[i, j] - factor * entry[k, j]
            left_rows[i] = left_rows[i] - factor * left_rows[k]
            right_rows[i] = right_rows[i] - factor * right_rows[k]
        for h in range(2):
            factor = next_columns[h][k] * inverse[k]
            for j in range(k + 1, 8):
                next_columns[h][j] = next_columns[h][j] - factor * entry[k, j]
            next_left[h] = next_left[h] - factor * left_rows[k]
            next_right[h] = next_right[h] - factor * right_rows[k]
    for h in range(2):
        nears[h, :, left_part] = next_left[h]
        nears[h, :, right_part] = next_right[h]

    def gathered(rows):
        low, high = rows[0], rows[4]
        for k in range(1, 4):
            low = jnp.where(sub % 4 == k, rows[k], low)
            high = jnp.where(sub % 4 == k, rows[4 + k], high)
        return joined(low, high)

    for work, turned, done, pivots, done_left, done_right in zip(
        works, turned_refs, done_refs, gathered(inverse), gathered(left_rows), gathered(right_rows)
    ):
        f1, f2, f3 = split_three(jnp.where(lane >= start + 16, done_left * pivots, 0.0))
        d1, d2, d3 = split_three(jnp.concatenate([done_left, done_right], axis=1))
        turned[...] = jnp.concatenate([f1, f1, f2, f1, f2, f3], axis=0).T.reshape(-1, 8, 48)
        done[...] = jnp.concatenate([d1, d2, d1, d3, d2, d1], axis=0).astype(BF16)
        root = jnp.sqrt(pivots)
        work[b, :, left_part] = done_left * root
        work[b, :, right_part] = done_right * root


def accurate(left, right):
    return lax.dot_general(
        left, right, (((1,), (1,)), ((), ())), precision=lax.Precision.HIGHEST, preferred_element_type=F32
    )


def modes_kernel(
    fields, gram, north, south, west, east, modes, forward, backward,
    body, work_one, work_two, splat, near, turned_one, turned_two, done_one, done_two, weights, first_column, plain, lower, left, right, operators,
    load_sem, store_sem,
):
    works, turned, done = (work_one, work_two), (turned_one, turned_two), (done_one, done_two)
    main = pl.ds(0, LANES)
    inner = pl.ds(1, ROWS)
    loads = [
        pltpu.make_async_copy(fields.at[:, :, :, main], body.at[:, inner, pl.ds(0, COLS), :], load_sem.at[0]),
        pltpu.make_async_copy(north, body.at[:, 0, pl.ds(0, COLS), :], load_sem.at[1]),
        pltpu.make_async_copy(south, body.at[:, ROWS + 1, pl.ds(0, COLS), :], load_sem.at[2]),
        pltpu.make_async_copy(fields.at[:, :, 0, main], first_column, load_sem.at[3]),
        pltpu.make_async_copy(east, body.at[:, inner, COLS, :], load_sem.at[4]),
    ]
    for copy in loads:
        copy.start()

    for work, (matrix, extended) in zip(works, unfolded(gram[...])):
        work[:, :, 0:LANES] = matrix.reshape(-1, 8, LANES)
        work[:, :, LANES : 2 * LANES] = extended.reshape(-1, 8, LANES)

    upper = iota((8, LANES), 0) < 4
    for part in range(0, 2 * LANES, LANES):
        first, second = [work[0, :, part : part + LANES] for work in works]
        near[0, :, part : part + LANES] = jnp.where(upper, first, pltpu.roll(second, 4, 0))
        near[1, :, part : part + LANES] = jnp.where(upper, pltpu.roll(first, 4, 0), second)
    for ref in turned + done:
        ref[...] = jnp.zeros_like(ref)

    for phase in range(4):

        def step(b, carry):
            eliminate(b, works, splat, near, turned, done, phase * 32)
            return carry

        lax.fori_loop(phase * 4, phase * 4 + 4, step, 0)

    row, lane = iota((LANES, LANES), 0), iota((LANES, LANES), 1)

    def parts(c):
        factor, extended = flat(works[c][:, :, 0:LANES]), flat(works[c][:, :, LANES : 2 * LANES])
        corner = jnp.where((row == LANES - 1) & (lane == LANES - 1), 1.0 / factor, 0.0)
        return factor, extended, jnp.where(lane == LANES - 1, corner, extended)

    factor, extended, inverse = parts(0)
    mixing = inverse.T
    high = mixing.astype(BF16)
    low = (mixing - high.astype(F32)).astype(BF16)
    line = jnp.concatenate([high, low], axis=1)
    weights[...] = jnp.concatenate([line, line], axis=0)

    for copy in loads:
        copy.wait()

    def mixed(value):
        both = jnp.dot(split_pair(value), weights[...], preferred_element_type=F32)
        return both[:, :LANES] + both[:, LANES:]

    inner_cols, outer_cols = pl.ds(0, COLS - 1), pl.ds(1, COLS - 1)

    def stores(c):
        pieces = (
            (plain.at[c], modes.at[c]),
            (lower.at[c, pl.ds(0, ROWS)], modes.at[CHANNELS + c]),
            (lower.at[c, pl.ds(1, ROWS)], modes.at[2 * CHANNELS + c]),
            (right.at[c, :, inner_cols, :], modes.at[3 * CHANNELS + c, :, outer_cols, :]),
            (right.at[c], modes.at[4 * CHANNELS + c]),
        )
        return [pltpu.make_async_copy(*piece, store_sem.at[kind]) for kind, piece in enumerate(pieces)]

    def stored(kind):
        whole = modes.at[pl.ds(kind * CHANNELS, CHANNELS)]
        if kind == 3:
            whole = whole.at[:, :, outer_cols, :]
        return pltpu.make_async_copy(whole, whole, store_sem.at[kind])

    first_store = pltpu.make_async_copy(
        left, modes.at[pl.ds(3 * CHANNELS, CHANNELS), :, 0, :], load_sem.at[0]
    )
    def channel(c, carry):
        value = body[c, 1 : ROWS + 1, 0:COLS, :]
        pairs = body[c, 0 : ROWS + 1, 0:COLS, :] * body[c, 1 : ROWS + 2, 0:COLS, :]
        beside = value * body[c, 1 : ROWS + 1, 1 : COLS + 1, :]
        copies = stores(c)
        plain[c] = mixed(flat(value)).reshape((ROWS, COLS, LANES))
        copies[0].start()
        lower[c] = mixed(flat(pairs)).reshape((ROWS + 1, COLS, LANES))
        copies[1].start()
        copies[2].start()
        right[c] = mixed(flat(beside)).reshape((ROWS, COLS, LANES))
        copies[3].start()
        copies[4].start()
        return carry

    lax.fori_loop(0, CHANNELS, channel, 0, unroll=True)

    left[...] = mixed(flat(first_column[...] * west[...])).reshape((CHANNELS, ROWS, LANES))
    first_store.start()

    shifted = jnp.where(lane == LANES - 1, extended, pltpu.roll(factor, LANES - 1, 1))
    operators[0] = accurate(shifted, inverse)
    forward_store = pltpu.make_async_copy(operators.at[0], forward, load_sem.at[1])
    forward_store.start()
    factor, extended, inverse = parts(1)
    mixed_block = jnp.where(lane == 0, pltpu.roll(extended, 1, 1), pltpu.roll(factor, 1, 1))
    operators[1] = accurate(mixed_block, inverse)
    backward_store = pltpu.make_async_copy(operators.at[1], backward, load_sem.at[2])
    backward_store.start()
    for kind in range(5):
        stored(kind).wait()
    first_store.wait()
    forward_store.wait()
    backward_store.wait()


def modes_call(fields, gram, north, south, west, east):
    shape = (CHANNELS, ROWS, COLS, LANES)
    any_space = pl.BlockSpec(memory_space=pl.ANY)
    vmem = pl.BlockSpec(memory_space=pltpu.VMEM)
    return pl.pallas_call(
        modes_kernel,
        out_shape=[
            jax.ShapeDtypeStruct((5 * CHANNELS, ROWS, COLS, LANES), F32),
            jax.ShapeDtypeStruct((LANES, LANES), F32),
            jax.ShapeDtypeStruct((LANES, LANES), F32),
        ],
        in_specs=[pl.BlockSpec(memory_space=pltpu.HBM), vmem, any_space, any_space, vmem, any_space],
        out_specs=[any_space] * 3,
        scratch_shapes=[
            pltpu.VMEM((CHANNELS, ROWS + 2, COLS + 8, LANES), F32),
            pltpu.VMEM((LANES // 8, 8, 2 * LANES), F32),
            pltpu.VMEM((LANES // 8, 8, 2 * LANES), F32),
            pltpu.VMEM((2, 8, 8, LANES), F32),
            pltpu.VMEM((2, 8, 2 * LANES), F32),
            pltpu.VMEM((LANES // 8, 8, 48), F32),
            pltpu.VMEM((LANES // 8, 8, 48), F32),
            pltpu.VMEM((48, 2 * LANES), BF16),
            pltpu.VMEM((48, 2 * LANES), BF16),
            pltpu.VMEM((2 * LANES, 2 * LANES), BF16),
            pltpu.VMEM((CHANNELS, ROWS, LANES), F32),
            pltpu.VMEM(shape, F32),
            pltpu.VMEM((CHANNELS, ROWS + 1, COLS, LANES), F32),
            pltpu.VMEM((CHANNELS, ROWS, LANES), F32),
            pltpu.VMEM(shape, F32),
            pltpu.VMEM((2, LANES, LANES), F32),
            pltpu.SemaphoreType.DMA((5,)),
            pltpu.SemaphoreType.DMA((5,)),
        ],
        compiler_params=pltpu.CompilerParams(vmem_limit_bytes=48 << 20),
    )(fields, gram, north, south, west, east)


def shards(fields):
    cells = pltpu.with_memory_space_constraint(fields.transpose(1, 2, 3, 0), pltpu.HBM)
    gram, north, south, west, east = gram_call(cells, lax.axis_size("lat"), lax.axis_size("lon"))
    return tuple(modes_call(cells, gram, north, south, west, east))


def solution(mesh):
    return jax.shard_map(
        shards,
        mesh=mesh,
        in_specs=(P(None, None, "lat", "lon"),),
        out_specs=(P(None, "lat", "lon", None), P(), P()),
        check_vma=False,
    )
```
